128 devices in a mesh: seq: 32 (over y, x, z_lo), mp: 4 (over z_hi, core).
Axes of the slice: x: 4, y: 4, z: 4 (z_hi: 2, z_lo: 2; z = z_hi * 2 + z_lo), core: 2. Of those that a mesh axis runs over, the one named last changes fastest.
Arguments:
- frames: bfloat16 [768, 250, 256], P('seq'), may hold values from -7.5 to 7.5
- intra_qkv: bfloat16 [256, 3, 256], P(None, None, 'mp'), may hold values from -20 to 20
- intra_out: bfloat16 [256, 256], P('mp'), may hold values from -0.375 to 0.375
- intra_up: bfloat16 [256, 1024], P(None, 'mp'), may hold values from -0.375 to 0.375
- intra_down: bfloat16 [1024, 256], P('mp'), may hold values from -0.1875 to 0.1875
- inter_qkv: bfloat16 [256, 3, 256], P(None, None, 'mp'), may hold values from -20 to 20
- inter_out: bfloat16 [256, 256], P('mp'), may hold values from -0.375 to 0.375
- inter_up: bfloat16 [256, 1024], P(None, 'mp'), may hold values from -0.375 to 0.375
- inter_down: bfloat16 [1024, 256], P('mp'), may hold values from -0.1875 to 0.1875
Outputs:
- margin_sum: bfloat16 [96000, 256], P('seq')
The draws below stay inside these ranges and needn't reach their ends.
All inputs are finite; a program needn't handle non-finite values.
Results may differ from the reference program's by a relative error of at most 0.014.
Values may be sent and summed in bfloat16 or wider, within the bound.
No kernel may reach another device: no remote copies, remote signals or barrier semaphores. Data moves between devices by JAX's collectives and lax.ppermute only.
A program may use at most 128 MiB of HBM per device.

```python
import jax
import jax.numpy as jnp
from jax import lax

D = 256
HEADS = 8
HD = 32
FF = 1024
K = 250
STRETCHES = 768


def draw_frames(key, part):
    keyed = jax.random.fold_in(key, 11)
    first = jax.random.fold_in(keyed, 0)
    values = jax.random.normal(first, (STRETCHES, K, D), jnp.float32)
    return jnp.clip(values, -7.5, 7.5).astype(jnp.bfloat16)


def attention_weights(key, salt):
    keyed = jax.random.fold_in(key, salt)
    first = jax.random.fold_in(keyed, 0)
    weights = jax.random.normal(first, (D, 3, D), jnp.float32) * D ** (-0.5)
    return jnp.clip(weights, -20.0, 20.0).astype(jnp.bfloat16)


def draw_intra_qkv(key, part):
    return attention_weights(key, 23)


def draw_inter_qkv(key, part):
    return attention_weights(key, 37)


def level_of(rng, shape, cuts, low, largest):
    gain, own = 1.0, jax.random.fold_in(rng, 6)
    for position, parts in cuts:
        steps = jnp.exp(jax.random.uniform(jax.random.fold_in(own, position), (parts,), jnp.float32, low / len(cuts), largest / len(cuts)))
        gain = gain * jnp.repeat(steps, shape[position] // parts).reshape([-1 if axis == position else 1 for axis in range(len(shape))])
    return gain


def centred(own_key, extent, width, most, cuts=(), dtype=jnp.bfloat16):
    result = jax.random.normal(own_key, extent, jnp.float32) * width
    if len(cuts) > 0:
        result = level_of(own_key, extent, cuts, -0.22, 0.18) * result
    return jnp.clip(result, min=-most, max=most).astype(dtype)


def setup_inputs(seed: int = 0) -> dict:
    streams_of = jax.random.split(jax.random.key(seed), 10)
    return {
        "frames": draw_frames(jax.random.fold_in(streams_of[9], 71), 0),
        "intra_qkv": draw_intra_qkv(jax.random.fold_in(streams_of[9], 71), 0),
        "intra_out": centred(streams_of[2], (D, D), D ** -0.5, 0.375, ((0, 4),)),
        "intra_up": centred(streams_of[3], (D, FF), D ** -0.5, 0.375, ((1, 4),)),
        "intra_down": centred(streams_of[4], (FF, D), FF ** -0.5, 0.1875, ((0, 4),)),
        "inter_qkv": draw_inter_qkv(jax.random.fold_in(streams_of[9], 71), 0),
        "inter_out": centred(streams_of[6], (D, D), D ** -0.5, 0.375, ((0, 4),)),
        "inter_up": centred(streams_of[7], (D, FF), D ** -0.5, 0.375, ((1, 4),)),
        "inter_down": centred(streams_of[8], (FF, D), FF ** -0.5, 0.1875, ((0, 4),)),
    }


def layer_norm(values):
    values = values.astype(jnp.float32)
    centre = values - lax.optimization_barrier(jnp.mean(values, axis=-1, keepdims=True))
    spread = lax.optimization_barrier(jnp.mean(centre * centre, axis=-1, keepdims=True))
    return (centre * lax.rsqrt(spread + 1e-05)).astype(jnp.bfloat16)

def attend(query_rows, key_rows, value_rows):
    factor = HD ** (-0.5)
    scores = jnp.einsum('bqhe,bkhe->bhqk', query_rows.astype(jnp.float32), key_rows.astype(jnp.float32)) * factor
    scores = scores - lax.optimization_barrier(jnp.max(scores, axis=-1, keepdims=True))
    weights = jnp.exp(scores)
    weights = (weights / lax.optimization_barrier(jnp.sum(weights, axis=-1, keepdims=True))).astype(jnp.bfloat16)
    return jnp.einsum('bhqk,bkhe->bqhe', weights.astype(jnp.float32), value_rows.astype(jnp.float32)).astype(jnp.bfloat16)

def transformer(stream, qkv_weight, out_weight, up_weight, down_weight):
    leading, within = (stream.shape[0], stream.shape[1])
    normed = layer_norm(stream)
    projected = jnp.einsum('bld,dtj->tblj', normed.astype(jnp.float32), qkv_weight.astype(jnp.float32)).astype(jnp.bfloat16)
    projected = projected.reshape(3, leading // 2, 2, within, HEADS, HD)
    attended = lax.map(lambda pieces: attend(pieces[0], pieces[1], pieces[2]), (projected[0], projected[1], projected[2]))
    attended = attended.reshape(leading, within, D)
    branch = jnp.einsum('bld,de->ble', attended.astype(jnp.float32), out_weight.astype(jnp.float32))
    middle = (stream.astype(jnp.float32) + branch).astype(jnp.bfloat16)
    normed = layer_norm(middle)
    hidden = jax.nn.relu(jnp.einsum('bld,df->blf', normed.astype(jnp.float32), up_weight.astype(jnp.float32))).astype(jnp.bfloat16)
    branch = jnp.einsum('blf,fd->bld', hidden.astype(jnp.float32), down_weight.astype(jnp.float32))
    return (middle.astype(jnp.float32) + branch).astype(jnp.bfloat16)

def reference(frames, intra_qkv, intra_out, intra_up, intra_down, inter_qkv, inter_out, inter_up, inter_down):
    stream = transformer(frames, intra_qkv, intra_out, intra_up, intra_down)
    across = transformer(jnp.transpose(stream, (1, 0, 2)), inter_qkv, inter_out, inter_up, inter_down)
    stream = jnp.transpose(across, (1, 0, 2))
    hop_len = K // 2
    tail_rows = stream[:, hop_len:]
    earlier = jnp.concatenate([jnp.zeros((1, hop_len, D), jnp.bfloat16), tail_rows[:-1]], axis=0)
    summed = stream[:, :hop_len].astype(jnp.float32) + earlier.astype(jnp.float32)
    return summed.astype(jnp.bfloat16).reshape(STRETCHES * hop_len, D)
```

```python
import jax
import jax.numpy as jnp
from jax import lax
from jax.experimental import pallas as pl
from jax.experimental.pallas import tpu as pltpu
from jax.sharding import PartitionSpec as P

HEADS = 8
HD = 32
K = 250
HALF = K // 2
D = 256
MP = 4
BF = jnp.bfloat16
F32 = jnp.float32
Q_SCALE = 1.4426950408889634 * HD ** (-0.5)
LOW = -1e30
VMEM_BYTES = 56 * 1024 * 1024


def params(**more):
    return pltpu.CompilerParams(vmem_limit_bytes=VMEM_BYTES, **more)


def dot(left, right, left_dim=1, right_dim=0):
    return lax.dot_general(
        left, right, (((left_dim,), (right_dim,)), ((), ())), preferred_element_type=F32
    )


def normed(values):
    centre = values - jnp.mean(values, axis=-1, keepdims=True)
    spread = jnp.mean(centre * centre, axis=-1, keepdims=True)
    return (centre * lax.rsqrt(spread + 1e-05)).astype(BF)


def pack_attention(qkv_ref, out_ref, packed_ref):
    for t in range(3):
        packed_ref[64 * t : 64 * t + 64, :] = qkv_ref[:, t, :].astype(F32).T.astype(BF)
    packed_ref[192:256, :] = out_ref[...]


def pack_rest(up1_ref, down1_ref, qkv_ref, out_ref, up2_ref, down2_ref, packed_ref):
    packed_ref[0:256, :] = up1_ref[...]
    packed_ref[256:512, :] = down1_ref[...]
    for t in range(3):
        packed_ref[512 + 64 * t : 576 + 64 * t, :] = qkv_ref[:, t, :].astype(F32).T.astype(BF)
    packed_ref[704:768, :] = out_ref[...]
    packed_ref[768:1024, :] = up2_ref[...]
    packed_ref[1024:1280, :] = down2_ref[...]


def put_attention_weights(shards, at, weights_ref):
    for k in range(MP):
        for t in range(4):
            weights_ref[t, 64 * k : 64 * k + 64, :] = shards[k][at + 64 * t : at + 64 * t + 64, :]


def project(rows, weights_ref, query_ref, key_ref, value_ref):
    query_ref[...] = (dot(weights_ref[0], rows, 1, 1) * Q_SCALE).astype(BF)
    keys = dot(rows, weights_ref[1], 1, 1).astype(BF)
    lane = lax.broadcasted_iota(jnp.int32, (rows.shape[0], 128), 1) // HD
    for h in range(HEADS):
        part = keys[:, 128 * (h // 4) : 128 * (h // 4) + 128]
        key_ref[h] = jnp.where(lane == h % 4, part, jnp.zeros_like(part))
    values = dot(weights_ref[2], rows, 1, 1).astype(BF)
    for h in range(HEADS):
        value_ref[h, 0:HD, :] = values[HD * h : HD * h + HD, :]
        value_ref[h, HD:48, :] = jnp.ones((48 - HD, rows.shape[0]), BF)


def attend(columns, query_ref, key_ref, value_ref, attended_ref, valid=None):
    def scores(h):
        at = 128 * (h // 4)
        found = dot(key_ref[h], query_ref[at : at + 128, columns])
        return found if valid is None else jnp.where(valid, found, LOW)

    following = scores(0)
    for h in range(HEADS):
        current = following
        if h + 1 < HEADS:
            following = scores(h + 1)
        top = jnp.max(current, axis=0, keepdims=True)
        weights = jnp.exp2(current - top).astype(BF)
        mixed = dot(value_ref[h], weights)
        attended_ref[HD * h : HD * h + HD, columns] = mixed[0:HD] * (1.0 / mixed[HD : HD + 1])


def intra_attention(x_ref, w0, w1, w2, w3, o_ref, weights_ref, query_ref, key_ref, value_ref, attended_ref):
    @pl.when(pl.program_id(0) == 0)
    def _():
        put_attention_weights((w0, w1, w2, w3), 0, weights_ref)

    x = x_ref[0].astype(F32)
    project(normed(x), weights_ref, query_ref, key_ref, value_ref)
    place = lax.broadcasted_iota(jnp.int32, (2 * 128, 2 * 128), 0)
    valid = (place % 128) < HALF
    attend(slice(0, 256), query_ref, key_ref, value_ref, attended_ref, valid)
    attended = attended_ref[...].T.astype(BF)
    o_ref[0] = (x + dot(attended, weights_ref[3])).astype(BF)


def feed_forward(middle, up, down):
    middle = middle.astype(F32)
    rows = normed(middle)
    total = middle
    for u, d in zip(up, down):
        hidden = jnp.maximum(dot(rows, u), 0.0).astype(BF)
        total = total + dot(hidden, d)
    return total.astype(BF)


def intra_feed_forward(x_ref, w0, w1, w2, w3, o_ref):
    shards = (w0, w1, w2, w3)
    o_ref[0] = feed_forward(
        x_ref[0], [w[0:256, :] for w in shards], [w[256:512, :] for w in shards]
    )


def inter_layer(x_ref, w0, w1, w2, w3, o_ref, weights_ref, query_ref, key_ref, value_ref, attended_ref, later_ref):
    shards = (w0, w1, w2, w3)
    step = pl.program_id(0)

    @pl.when(step == 0)
    def _():
        put_attention_weights(shards, 512, weights_ref)

    x = x_ref[0].astype(F32)
    project(normed(x), weights_ref, query_ref, key_ref, value_ref)

    def block(i, carry):
        columns = pl.ds(pl.multiple_of(i * 256, 256), 256)
        attend(columns, query_ref, key_ref, value_ref, attended_ref)
        return carry

    lax.fori_loop(0, x.shape[0] // 256, block, 0)
    attended = attended_ref[...].T.astype(BF)
    middle = (x + dot(attended, weights_ref[3])).astype(BF)
    done = feed_forward(
        middle, [w[768:1024, :] for w in shards], [w[1024:1280, :] for w in shards]
    ).astype(F32)

    @pl.when(step == 0)
    def _():
        later_ref[128:768, :] = done[0:640]
        turned = pltpu.roll(done[640:768], 1, 0)
        first = lax.broadcasted_iota(jnp.int32, turned.shape, 0) == 0
        later_ref[0:128, :] = jnp.where(first, 0.0, turned)

    @pl.when(step == 1)
    def _():
        o_ref[...] = (done + later_ref[...]).astype(BF)


def whole(shape):
    return pl.BlockSpec(shape, lambda i: (0,) * len(shape))


def attention_scratch(length):
    return [
        pltpu.VMEM((4, D, D), BF),
        pltpu.VMEM((D, length), BF),
        pltpu.VMEM((HEADS, length, 128), BF),
        pltpu.VMEM((HEADS, 48, length), BF),
        pltpu.VMEM((D, length), F32),
    ]


def by(shard, k):
    return lax.ppermute(shard, "mp", [(i, i ^ k) for i in range(MP)])


def on_device(
    frames, intra_qkv, intra_out, intra_up, intra_down, inter_qkv, inter_out, inter_up, inter_down
):
    seq_count = lax.axis_size("seq")
    mine = lax.axis_index("mp")
    spans = frames.shape[0] // MP
    total = spans * seq_count * MP

    first = pl.pallas_call(
        pack_attention, out_shape=jax.ShapeDtypeStruct((256, D), BF), name="pack_first"
    )(intra_qkv, intra_out)
    first = [first, by(first, 1), by(first, 2), by(first, 3)]
    rest = pl.pallas_call(
        pack_rest, out_shape=jax.ShapeDtypeStruct((1280, D), BF), name="pack_rest"
    )(intra_up, intra_down, inter_qkv, inter_out, inter_up, inter_down)
    across = by(rest, 2)
    rest = [rest, by(rest, 1), across, by(across, 1)]

    own = lax.dynamic_slice_in_dim(frames, mine * spans, spans, 0)
    own = jnp.pad(own.reshape(spans, 2, HALF, D), ((0, 0), (0, 0), (0, 3), (0, 0)))
    own = own.reshape(spans, 256, D)

    row_block = pl.BlockSpec((1, 256, D), lambda i: (i, 0, 0))
    middle = pl.pallas_call(
        intra_attention,
        out_shape=jax.ShapeDtypeStruct(own.shape, BF),
        grid=(spans,),
        in_specs=[row_block] + [whole((256, D))] * 4,
        out_specs=row_block,
        scratch_shapes=attention_scratch(256),
        compiler_params=params(),
        cost_estimate=pl.CostEstimate(flops=10**10, bytes_accessed=2 * 10**6, transcendentals=3 * 10**6),
        name="intra_attention",
    )(own, *first)
    stream = pl.pallas_call(
        intra_feed_forward,
        out_shape=jax.ShapeDtypeStruct(own.shape, BF),
        grid=(spans,),
        in_specs=[row_block] + [whole((512, D))] * 4,
        out_specs=row_block,
        compiler_params=params(),
        cost_estimate=pl.CostEstimate(flops=3 * 10**9, bytes_accessed=3 * 10**6, transcendentals=0),
        name="intra_feed_forward",
    )(middle, *rest)

    send = stream.reshape(spans, 2, MP, seq_count, D)
    send = jnp.transpose(send, (3, 2, 1, 0, 4)).reshape(seq_count * MP, 2 * spans, D)
    got = lax.all_to_all(send, ("seq", "mp"), split_axis=0, concat_axis=0, tiled=True)
    got = jnp.transpose(got.reshape(seq_count * MP, 2, spans, D), (1, 2, 0, 3))
    got = got.reshape(2, total, D)

    summed = pl.pallas_call(
        inter_layer,
        out_shape=jax.ShapeDtypeStruct((total, D), BF),
        grid=(2,),
        in_specs=[pl.BlockSpec((1, total, D), lambda i: (1 - i, 0, 0))] + [whole((1280, D))] * 4,
        out_specs=whole((total, D)),
        scratch_shapes=attention_scratch(total) + [pltpu.VMEM((total, D), F32)],
        compiler_params=params(),
        cost_estimate=pl.CostEstimate(flops=3 * 10**10, bytes_accessed=4 * 10**6, transcendentals=10**7),
        name="inter_layer",
    )(got, *rest)

    back = jnp.transpose(summed.reshape(spans, seq_count, MP, D), (1, 2, 0, 3))
    back = back.reshape(seq_count, MP * spans, D)
    back = lax.all_to_all(back, "seq", split_axis=0, concat_axis=0, tiled=True)
    back_across = by(back, 2)
    pieces = [back, by(back, 1), back_across, by(back_across, 1)]
    for bit in (1, 2):
        swapped = (mine & bit) > 0
        pieces = [jnp.where(swapped, pieces[k ^ bit], pieces[k]) for k in range(MP)]
    rows = jnp.transpose(jnp.stack(pieces), (2, 0, 1, 3)).reshape(MP * spans, MP * seq_count, D)
    return rows[:, :HALF].reshape(-1, D)


def solution(mesh):
    return jax.shard_map(
        on_device,
        mesh=mesh,
        in_specs=(
            P("seq", None, None),
            P(None, None, "mp"),
            P("mp", None),
            P(None, "mp"),
            P("mp", None),
            P(None, None, "mp"),
            P("mp", None),
            P(None, "mp"),
            P("mp", None),
        ),
        out_specs=P("seq", None),
        check_vma=False,
    )
```

```python
import jax
import jax.numpy as jnp
from jax import lax
from jax.experimental import pallas as pl
from jax.experimental.pallas import tpu as pltpu
from jax.sharding import PartitionSpec as P

HEADS = 8
HD = 32
K = 250
HALF = K // 2
D = 256
MP = 4
BF = jnp.bfloat16
F32 = jnp.float32
Q_SCALE = 1.4426950408889634 * HD ** (-0.5)
LOW = -1e30
VMEM_BYTES = 56 * 1024 * 1024


def params(**more):
    return pltpu.CompilerParams(vmem_limit_bytes=VMEM_BYTES, **more)


def dot(left, right, left_dim=1, right_dim=0):
    return lax.dot_general(
        left, right, (((left_dim,), (right_dim,)), ((), ())), preferred_element_type=F32
    )


def normed(values):
    centre = values - jnp.mean(values, axis=-1, keepdims=True)
    spread = jnp.mean(centre * centre, axis=-1, keepdims=True)
    return (centre * lax.rsqrt(spread + 1e-05)).astype(BF)


def pack_attention(qkv_ref, out_ref, packed_ref):
    for t in range(3):
        packed_ref[64 * t : 64 * t + 64, :] = qkv_ref[t].astype(F32).T.astype(BF)
    packed_ref[192:256, :] = out_ref[...]


def pack_rest(up1_ref, down1_ref, qkv_ref, out_ref, up2_ref, down2_ref, packed_ref):
    packed_ref[0:256, :] = up1_ref[...]
    packed_ref[256:512, :] = down1_ref[...]
    for t in range(3):
        packed_ref[512 + 64 * t : 576 + 64 * t, :] = qkv_ref[t].astype(F32).T.astype(BF)
    packed_ref[704:768, :] = out_ref[...]
    packed_ref[768:1024, :] = up2_ref[...]
    packed_ref[1024:1280, :] = down2_ref[...]


def put_attention_weights(shards, at, weights_ref):
    for k in range(MP):
        for t in range(4):
            weights_ref[t, 64 * k : 64 * k + 64, :] = shards[k][at + 64 * t : at + 64 * t + 64, :]


def project(rows, weights_ref, query_ref, key_ref, value_ref):
    query_ref[...] = (dot(weights_ref[0], rows, 1, 1) * Q_SCALE).astype(BF)
    keys = dot(rows, weights_ref[1], 1, 1).astype(BF)
    lane = lax.broadcasted_iota(jnp.int32, (rows.shape[0], 128), 1) // HD
    for h in range(HEADS):
        part = keys[:, 128 * (h // 4) : 128 * (h // 4) + 128]
        key_ref[h] = jnp.where(lane == h % 4, part, jnp.zeros_like(part))
    values = dot(weights_ref[2], rows, 1, 1).astype(BF)
    for h in range(HEADS):
        value_ref[h, 0:HD, :] = values[HD * h : HD * h + HD, :]
        value_ref[h, HD:48, :] = jnp.ones((48 - HD, rows.shape[0]), BF)


def attend(columns, query_ref, key_ref, value_ref, attended_ref):
    def scores(h):
        at = 128 * (h // 4)
        return dot(key_ref[h], query_ref[at : at + 128, columns])

    following = scores(0)
    for h in range(HEADS):
        current = following
        if h + 1 < HEADS:
            following = scores(h + 1)
        top = jnp.max(current, axis=0, keepdims=True)
        weights = jnp.exp2(current - top).astype(BF)
        mixed = dot(value_ref[h], weights)
        attended_ref[HD * h : HD * h + HD, columns] = mixed[0:HD] * (1.0 / mixed[HD : HD + 1])


def prepare(mine_ref, x_ref, n_ref, nq_ref, xq_ref, x_scratch, n_scratch):
    at = pl.multiple_of(mine_ref[0] * 32, 32)
    for u in range(x_ref.shape[0]):
        x = x_ref[u].astype(F32)
        centre = x - jnp.mean(x, axis=-1, keepdims=True)
        spread = jnp.mean(centre * centre, axis=-1, keepdims=True)
        for value, scratch in ((x, x_scratch), (centre * lax.rsqrt(spread + 1e-05), n_scratch)):
            scratch[u, 0:K, :] = value
            scratch[u, K:256, :] = jnp.zeros((256 - K, D), F32)
        late = n_scratch[u, HALF : HALF + 128, :]
        n_ref[u, 0:128, :] = n_scratch[u, 0:128, :].astype(BF)
        n_ref[u, 128:256, :] = late.astype(BF)
        for scratch, out_ref in ((x_scratch, xq_ref), (n_scratch, nq_ref)):
            out_ref[u, 0:32, :] = scratch[u, pl.ds(at, 32), :].astype(BF)
            late = scratch[u, HALF : HALF + 128, :]
            scratch[u, 0:128, :] = late
            out_ref[u, 32:64, :] = scratch[u, pl.ds(at, 32), :].astype(BF)


def intra_attention(n_ref, nq_ref, xq_ref, w0, w1, w2, w3, o_ref, weights_ref):
    @pl.when(pl.program_id(0) == 0)
    def _():
        put_attention_weights((w0, w1, w2, w3), 0, weights_ref)

    count = n_ref.shape[0]
    row = lax.broadcasted_iota(jnp.int32, (256, 256), 0)
    lane = lax.broadcasted_iota(jnp.int32, (256, 256), 1)
    valid = (row % 128) < HALF
    same = (row % 128) // HD == lane // 64
    keys, queries, values = [], [], []
    for u in range(count):
        rows = n_ref[u]
        few = nq_ref[u]
        keys.append(dot(rows, weights_ref[1], 1, 1).astype(BF))
        query = dot(weights_ref[0], jnp.concatenate([few] * 4, axis=0), 1, 1) * Q_SCALE
        queries.append(jnp.where(same, query, 0.0).astype(BF))
        values.append(dot(weights_ref[2], rows, 1, 1).astype(BF))
    parts = [(u, g) for u in range(count) for g in range(2)]

    def scores(u, g):
        part = slice(128 * g, 128 * g + 128)
        return jnp.where(valid, dot(keys[u][:, part], queries[u][part]), LOW)

    following = scores(*parts[0])
    found = []
    ones = jnp.ones((16, 256), BF)
    for at, (u, g) in enumerate(parts):
        current = following
        if at + 1 < len(parts):
            following = scores(*parts[at + 1])
        top = jnp.max(current, axis=0, keepdims=True)
        weights = jnp.exp2(current - top).astype(BF)
        mixed = dot(jnp.concatenate([values[u][128 * g : 128 * g + 128], ones], axis=0), weights)
        mixed = jnp.where(same[0:128], mixed[0:128] * (1.0 / mixed[128:129]), 0.0)
        mixed = (mixed[:, 0:128] + mixed[:, 128:256]).T
        found.append((mixed[0:64] + mixed[64:128]).astype(BF))
    attended = jnp.concatenate(
        [jnp.concatenate(found[2 * u : 2 * u + 2], axis=1) for u in range(count)], axis=0
    )
    branch = dot(attended, weights_ref[3])
    for u in range(count):
        o_ref[u] = (xq_ref[u].astype(F32) + branch[64 * u : 64 * u + 64]).astype(BF)


def feed_forward(middle, up, down):
    middle = middle.astype(F32)
    rows = normed(middle)
    total = middle
    for u, d in zip(up, down):
        hidden = jnp.maximum(dot(rows, u), 0.0).astype(BF)
        total = total + dot(hidden, d)
    return total.astype(BF)


def swapped(outer, inner):
    size = outer * inner
    to = lax.broadcasted_iota(jnp.int32, (size, size), 0)
    source = lax.broadcasted_iota(jnp.int32, (size, size), 1)
    return jnp.where(source % inner * outer + source // inner == to, 1.0, 0.0).astype(BF)


def intra_feed_forward(x_ref, w0, w1, w2, w3, o_ref, rows_ref):
    shards = (w0, w1, w2, w3)
    count = x_ref.shape[0]
    up = [w[0:256, :] for w in shards]
    down = [w[256:512, :] for w in shards]
    for at in range(0, count, 8):
        middle = x_ref[at : at + 8].reshape(512, D)
        rows_ref[64 * at : 64 * at + 512, :] = feed_forward(middle, up, down).astype(F32)
    turn = swapped(2 * count, 8)
    for part in range(4):
        taken = [
            rows_ref[64 * u + 32 * half + 8 * part : 64 * u + 32 * half + 8 * part + 8, :]
            for half in range(2)
            for u in range(count)
        ]
        size = 16 * count
        o_ref[size * part : size * part + size, :] = dot(
            turn, jnp.concatenate(taken, axis=0).astype(BF)
        ).astype(BF)


def inter_layer(x_ref, w0, w1, w2, w3, o_ref, weights_ref, query_ref, key_ref, value_ref, attended_ref, later_ref):
    shards = (w0, w1, w2, w3)
    step = pl.program_id(0)

    @pl.when(step == 0)
    def _():
        put_attention_weights(shards, 512, weights_ref)

    x = x_ref[:, 0].astype(F32).reshape(o_ref.shape)
    project(normed(x), weights_ref, query_ref, key_ref, value_ref)

    def block(i, carry):
        columns = pl.ds(pl.multiple_of(i * 256, 256), 256)
        attend(columns, query_ref, key_ref, value_ref, attended_ref)
        return carry

    lax.fori_loop(0, x.shape[0] // 256, block, 0)
    attended = attended_ref[...].T.astype(BF)
    middle = (x + dot(attended, weights_ref[3])).astype(BF)
    done = feed_forward(
        middle, [w[768:1024, :] for w in shards], [w[1024:1280, :] for w in shards]
    ).astype(F32)

    @pl.when(step == 0)
    def _():
        first = lax.broadcasted_iota(jnp.int32, done.shape, 0) == 0
        later_ref[...] = jnp.where(first, 0.0, pltpu.roll(done, 1, 0))

    @pl.when(step == 1)
    def _():
        o_ref[...] = (done + later_ref[...]).astype(BF)


def assemble(mine_ref, p0, p1, p2, p3, o_ref, rows_ref):
    turn = swapped(32, 8)
    for k, piece in enumerate((p0, p1, p2, p3)):
        at = pl.multiple_of((mine_ref[0] ^ k) * 32, 32)
        for part in range(3):
            taken = [piece[s, 8 * part : 8 * part + 8, :].astype(F32) for s in range(32)]
            rows = dot(turn, jnp.concatenate(taken, axis=0).astype(BF)).astype(BF)
            for u in range(8):
                rows_ref[8 * part + u, pl.ds(at, 32), :] = rows[32 * u : 32 * u + 32]
    to = lax.broadcasted_iota(jnp.int32, (128, 256), 0)
    source = lax.broadcasted_iota(jnp.int32, (128, 256), 1)
    for b in range(24):
        place = to + 3 * b
        place = jnp.where(place < HALF, place, place + 3)
        pick = jnp.where(place == source, 1.0, 0.0).astype(BF)
        rows = jnp.concatenate([rows_ref[b], rows_ref[min(b + 1, 23)]], axis=0)
        size = min(128, 3000 - 128 * b)
        o_ref[128 * b : 128 * b + size, :] = dot(pick, rows)[0:size].astype(BF)


def whole(shape):
    return pl.BlockSpec(shape, lambda i, *_: (0,) * len(shape))


def attention_scratch(length):
    return [
        pltpu.VMEM((4, D, D), BF),
        pltpu.VMEM((D, length), BF),
        pltpu.VMEM((HEADS, length, 128), BF),
        pltpu.VMEM((HEADS, 48, length), BF),
        pltpu.VMEM((D, length), F32),
    ]


def by(shard, k):
    return lax.ppermute(shard, "mp", [(i, i ^ k) for i in range(MP)])


def on_device(
    frames, intra_qkv, intra_out, intra_up, intra_down, inter_qkv, inter_out, inter_up, inter_down
):
    seq_count = lax.axis_size("seq")
    mine = lax.axis_index("mp").reshape(1)
    count = frames.shape[0]
    total = count * seq_count

    first = pl.pallas_call(
        pack_attention, out_shape=jax.ShapeDtypeStruct((256, D), BF), name="pack_first"
    )(jnp.transpose(intra_qkv, (1, 0, 2)), intra_out)
    across = by(first, 2)
    beside = by(first, 1)
    first = [first, beside, across, by(across, 1)]
    later = (intra_up, intra_down, jnp.transpose(inter_qkv, (1, 0, 2)), inter_out, inter_up, inter_down)
    *later, first[1] = lax.optimization_barrier((*later, beside))
    rest = pl.pallas_call(
        pack_rest, out_shape=jax.ShapeDtypeStruct((1280, D), BF), name="pack_rest"
    )(*later)
    across = by(rest, 2)
    rest = [rest, by(rest, 1), across, by(across, 1)]

    group = 4

    def blocks(rows):
        return pl.BlockSpec((group, rows, D), lambda i, *_: (i, 0, 0))

    few = jax.ShapeDtypeStruct((count, 64, D), BF)
    rows, few_rows, few_frames = pl.pallas_call(
        prepare,
        out_shape=(jax.ShapeDtypeStruct((count, 256, D), BF), few, few),
        grid_spec=pltpu.PrefetchScalarGridSpec(
            num_scalar_prefetch=1,
            grid=(count // group,),
            in_specs=[blocks(K)],
            out_specs=[blocks(256), blocks(64), blocks(64)],
            scratch_shapes=[pltpu.VMEM((group, 256, D), F32)] * 2,
        ),
        compiler_params=params(),
        cost_estimate=pl.CostEstimate(flops=10**7, bytes_accessed=8 * 10**6, transcendentals=10**4),
        name="prepare",
    )(mine, frames)
    middle = pl.pallas_call(
        intra_attention,
        out_shape=few,
        grid=(count // group,),
        in_specs=[blocks(256), blocks(64), blocks(64)] + [whole((256, D))] * 4,
        out_specs=blocks(64),
        scratch_shapes=[pltpu.VMEM((4, D, D), BF)],
        compiler_params=params(),
        cost_estimate=pl.CostEstimate(flops=10**10, bytes_accessed=4 * 10**6, transcendentals=3 * 10**6),
        name="intra_attention",
    )(rows, few_rows, few_frames, *first)
    send = pl.pallas_call(
        intra_feed_forward,
        out_shape=jax.ShapeDtypeStruct((64 * count, D), BF),
        grid=(1,),
        in_specs=[whole((count, 64, D))] + [whole((512, D))] * 4,
        out_specs=whole((64 * count, D)),
        scratch_shapes=[pltpu.VMEM((64 * count, D), F32)],
        compiler_params=params(),
        cost_estimate=pl.CostEstimate(flops=3 * 10**9, bytes_accessed=3 * 10**6, transcendentals=0),
        name="intra_feed_forward",
    )(middle, *rest)

    send = send.reshape(seq_count, 2 * count, D)
    got = lax.all_to_all(send, "seq", split_axis=0, concat_axis=0, tiled=True)
    got = got.reshape(seq_count, 2, count, D)

    summed = pl.pallas_call(
        inter_layer,
        out_shape=jax.ShapeDtypeStruct((total, D), BF),
        grid=(2,),
        in_specs=[pl.BlockSpec((seq_count, 1, count, D), lambda i: (0, 1 - i, 0, 0))]
        + [whole((1280, D))] * 4,
        out_specs=whole((total, D)),
        scratch_shapes=attention_scratch(total) + [pltpu.VMEM((total, D), F32)],
        compiler_params=params(),
        cost_estimate=pl.CostEstimate(flops=3 * 10**10, bytes_accessed=4 * 10**6, transcendentals=10**7),
        name="inter_layer",
    )(got, *rest)

    back = summed.reshape(seq_count, count, D)
    back = lax.all_to_all(back, "seq", split_axis=0, concat_axis=0, tiled=True)
    across = by(back, 2)
    pieces = [back, by(back, 1), across, by(across, 1)]
    return pl.pallas_call(
        assemble,
        out_shape=jax.ShapeDtypeStruct((HALF * count, D), BF),
        grid_spec=pltpu.PrefetchScalarGridSpec(
            num_scalar_prefetch=1,
            grid=(1,),
            in_specs=[whole(back.shape)] * 4,
            out_specs=whole((HALF * count, D)),
            scratch_shapes=[pltpu.VMEM((count, 128, D), BF)],
        ),
        compiler_params=params(),
        cost_estimate=pl.CostEstimate(flops=10**9, bytes_accessed=4 * 10**6, transcendentals=0),
        name="assemble",
    )(mine, *pieces)


def solution(mesh):
    return jax.shard_map(
        on_device,
        mesh=mesh,
        in_specs=(
            P("seq", None, None),
            P(None, None, "mp"),
            P("mp", None),
            P(None, "mp"),
            P("mp", None),
            P(None, None, "mp"),
            P("mp", None),
            P(None, "mp"),
            P("mp", None),
        ),
        out_specs=P("seq", None),
        check_vma=False,
    )
```

```python
import functools

import jax
import jax.numpy as jnp
from jax import lax
from jax.experimental import pallas as pl
from jax.experimental.pallas import tpu as pltpu
from jax.sharding import PartitionSpec as P

HEADS = 8
HD = 32
K = 250
HALF = K // 2
D = 256
MP = 4
BF = jnp.bfloat16
F32 = jnp.float32
Q_SCALE = 1.4426950408889634 * HD ** (-0.5)
LOW = -1e30
IN_VMEM = pl.BlockSpec(memory_space=pltpu.VMEM)


def params(mebibytes):
    return pltpu.CompilerParams(vmem_limit_bytes=mebibytes * 1024 * 1024)


def dot(left, right, left_dim=1, right_dim=0):
    return lax.dot_general(
        left, right, (((left_dim,), (right_dim,)), ((), ())), preferred_element_type=F32
    )


def normed(values):
    centre = values - jnp.mean(values, axis=-1, keepdims=True)
    spread = jnp.mean(centre * centre, axis=-1, keepdims=True)
    return (centre * lax.rsqrt(spread + 1e-05)).astype(BF)


def put_attention_weights(shards, weights_ref):
    for k in range(MP):
        for t in range(weights_ref.shape[0]):
            weights_ref[t, 64 * k : 64 * k + 64, :] = shards[k][64 * t : 64 * t + 64, :]


def project(rows, weights_ref, query_ref, key_ref, value_ref):
    query_ref[...] = (dot(weights_ref[0], rows, 1, 1) * Q_SCALE).astype(BF)
    keys = dot(rows, weights_ref[1], 1, 1).astype(BF)
    lane = lax.broadcasted_iota(jnp.int32, (rows.shape[0], 128), 1) // HD
    for h in range(HEADS):
        part = keys[:, 128 * (h // 4) : 128 * (h // 4) + 128]
        key_ref[h] = jnp.where(lane == h % 4, part, jnp.zeros_like(part))
    values = dot(weights_ref[2], rows, 1, 1).astype(BF)
    for h in range(HEADS):
        value_ref[h, 0:HD, :] = values[HD * h : HD * h + HD, :]
        value_ref[h, HD:48, :] = jnp.ones((48 - HD, rows.shape[0]), BF)


def attend(columns, query_ref, key_ref, value_ref, attended_ref):
    def scores(h):
        at = 128 * (h // 4)
        return dot(key_ref[h], query_ref[at : at + 128, columns])

    following = scores(0)
    for h in range(HEADS):
        current = following
        if h + 1 < HEADS:
            following = scores(h + 1)
        top = jnp.max(current, axis=0, keepdims=True)
        weights = jnp.exp2(current - top).astype(BF)
        mixed = dot(value_ref[h], weights)
        attended_ref[HD * h : HD * h + HD, columns] = mixed[0:HD] * (1.0 / mixed[HD : HD + 1])


def swapped(outer, bits):
    inner = 1 << bits
    size = outer * inner
    to = lax.broadcasted_iota(jnp.int32, (size, size), 0)
    source = lax.broadcasted_iota(jnp.int32, (size, size), 1)
    return jnp.where((source & (inner - 1)) * outer + (source >> bits) == to, 1.0, 0.0).astype(BF)


def pack(*refs):
    sources, packed_ref = refs[:-1], refs[-1]
    at = 0
    for source in sources:
        packed_ref[at : at + source.shape[0], :] = source[...]
        at += source.shape[0]


def prepare(mine_ref, x_ref, n_ref, xq_ref, turn_ref):
    count = x_ref.shape[1]
    turn_ref[...] = swapped(count, 4).T

    def put(to, x):
        rows = normed(x.astype(F32).reshape(16 * count, D))
        rows = dot(turn_ref[...], rows).astype(BF)
        for u in range(count):
            n_ref[u, pl.ds(to, 16), :] = rows[16 * u : 16 * u + 16]

    def early(b, carry):
        at = pl.multiple_of(b * 16, 16)
        put(at, x_ref[pl.ds(at, 16)])
        return carry

    def late(b, carry):
        at = pl.multiple_of(b * 16, 16)
        put(128 + at, x_ref[pl.ds(HALF + at, 16)])
        return carry

    lax.fori_loop(0, 8, early, 0)
    lax.fori_loop(0, 7, late, 0)
    put(240, jnp.concatenate([x_ref[HALF + 112 : K], x_ref[K - 3 : K]], axis=0))

    def residual(j, carry):
        r = mine_ref[0] * 32 + j
        xq_ref[0, j] = x_ref[r]
        xq_ref[1, j] = x_ref[jnp.minimum(HALF + r, K - 1)]
        return carry

    lax.fori_loop(0, 32, residual, 0)


def intra_attention(mine_ref, n_ref, w0, w1, w2, w3, o_ref, weights_ref):
    @pl.when(pl.program_id(0) == 0)
    def _():
        put_attention_weights((w0, w1, w2, w3), weights_ref)

    own = pl.multiple_of(mine_ref[0] * 32, 32)
    count = n_ref.shape[0]
    row = lax.broadcasted_iota(jnp.int32, (256, 256), 0)
    lane = lax.broadcasted_iota(jnp.int32, (256, 256), 1)
    valid = (row % 128) < HALF
    same = (row % 128) // HD == lane // 64
    keys, queries, values = [], [], []
    for u in range(count):
        rows = n_ref[u]
        few = jnp.concatenate(
            [n_ref[u, pl.ds(own, 32), :], n_ref[u, pl.ds(128 + own, 32), :]], axis=0
        )
        keys.append(dot(rows, weights_ref[1], 1, 1).astype(BF))
        query = dot(weights_ref[0], jnp.concatenate([few] * 4, axis=0), 1, 1) * Q_SCALE
        queries.append(jnp.where(same, query, 0.0).astype(BF))
        values.append(dot(weights_ref[2], rows, 1, 1).astype(BF))
    parts = [(u, g) for u in range(count) for g in range(2)]

    def scores(u, g):
        part = slice(128 * g, 128 * g + 128)
        return jnp.where(valid, dot(keys[u][:, part], queries[u][part]), LOW)

    following = scores(*parts[0])
    found = []
    ones = jnp.ones((16, 256), BF)
    for at, (u, g) in enumerate(parts):
        current = following
        if at + 1 < len(parts):
            following = scores(*parts[at + 1])
        top = jnp.max(current, axis=0, keepdims=True)
        weights = jnp.exp2(current - top).astype(BF)
        mixed = dot(jnp.concatenate([values[u][128 * g : 128 * g + 128], ones], axis=0), weights)
        mixed = jnp.where(same[0:128], mixed[0:128] * (1.0 / mixed[128:129]), 0.0)
        mixed = (mixed[:, 0:128] + mixed[:, 128:256]).T
        found.append((mixed[0:64] + mixed[64:128]).astype(BF))
    for u in range(count):
        o_ref[u] = jnp.concatenate(found[2 * u : 2 * u + 2], axis=1)


def feed_forward(middle, up, down):
    middle = middle.astype(F32)
    rows = normed(middle)
    total = middle
    for u, d in zip(up, down):
        hidden = jnp.maximum(dot(rows, u), 0.0).astype(BF)
        total = total + dot(hidden, d)
    return total.astype(BF)


def intra_feed_forward(a0_ref, a1_ref, xq_ref, w0, w1, w2, w3, o_ref):
    shards = (w0, w1, w2, w3)
    count = 2 * a0_ref.shape[0]
    out = jnp.concatenate([w[768:832, :] for w in shards], axis=0)
    up = [w[832:1088, :] for w in shards]
    down = [w[1088:1344, :] for w in shards]
    turn = swapped(count, 3)
    for half in range(2):
        for pair in range(2):
            rows = []
            for at in (32 * half + 16 * pair, 32 * half + 16 * pair + 8):
                taken = [
                    ref[u, at : at + 8, :].astype(F32)
                    for ref in (a0_ref, a1_ref)
                    for u in range(count // 2)
                ]
                rows.append(dot(turn, jnp.concatenate(taken, axis=0).astype(BF)).astype(BF))
            attended = jnp.concatenate(rows, axis=0)
            part = slice(16 * pair, 16 * pair + 16)
            x = xq_ref[half, part].astype(F32).reshape(16 * count, D)
            middle = (x + dot(attended, out)).astype(BF)
            done = feed_forward(middle, up, down).astype(F32)
            o_ref[part, half] = done.reshape(16, count, D).astype(BF)


def inter_layer(x_ref, w0, w1, w2, w3, o_ref, weights_ref, query_ref, key_ref, value_ref, attended_ref):
    shards = (w0, w1, w2, w3)
    put_attention_weights(shards, weights_ref)
    for half in (1, 0):
        x = x_ref[:, half].astype(F32).reshape(o_ref.shape)
        project(normed(x), weights_ref, query_ref, key_ref, value_ref)

        def block(i, carry):
            columns = pl.ds(pl.multiple_of(i * 256, 256), 256)
            attend(columns, query_ref, key_ref, value_ref, attended_ref)
            return carry

        lax.fori_loop(0, x.shape[0] // 256, block, 0)
        attended = attended_ref[...].T.astype(BF)
        middle = (x + dot(attended, weights_ref[3])).astype(BF)
        done = feed_forward(
            middle, [w[256:512, :] for w in shards], [w[512:768, :] for w in shards]
        )
        if half == 1:
            first = lax.broadcasted_iota(jnp.int32, done.shape, 0) == 0
            o_ref[...] = jnp.where(first, 0.0, pltpu.roll(done.astype(F32), 1, 0)).astype(BF)
        else:
            o_ref[...] = (done.astype(F32) + o_ref[...].astype(F32)).astype(BF)


def assemble(mine_ref, p0, p1, p2, p3, o_ref, rows_ref):
    turn = swapped(32, 3)
    for k, piece in enumerate((p0, p1, p2, p3)):
        at = pl.multiple_of((mine_ref[0] ^ k) * 32, 32)
        for part in range(3):
            taken = [piece[s, 8 * part : 8 * part + 8, :].astype(F32) for s in range(32)]
            rows = dot(turn, jnp.concatenate(taken, axis=0).astype(BF)).astype(BF)
            for u in range(8):
                rows_ref[8 * part + u, pl.ds(at, 32), :] = rows[32 * u : 32 * u + 32]
    to = lax.broadcasted_iota(jnp.int32, (128, 256), 0)
    source = lax.broadcasted_iota(jnp.int32, (128, 256), 1)
    for b in range(24):
        place = to + 3 * b
        place = jnp.where(place < HALF, place, place + 3)
        pick = jnp.where(place == source, 1.0, 0.0).astype(BF)
        rows = jnp.concatenate([rows_ref[b], rows_ref[min(b + 1, 23)]], axis=0)
        size = min(128, 3000 - 128 * b)
        o_ref[128 * b : 128 * b + size, :] = dot(pick, rows)[0:size].astype(BF)


def whole(shape):
    return pl.BlockSpec(shape, lambda i, *_: (0,) * len(shape))


def attention_scratch(length):
    return [
        pltpu.VMEM((4, D, D), BF),
        pltpu.VMEM((D, length), BF),
        pltpu.VMEM((HEADS, length, 128), BF),
        pltpu.VMEM((HEADS, 48, length), BF),
        pltpu.VMEM((D, length), F32),
    ]


def by(shard, k):
    return lax.ppermute(shard, "mp", [(i, i ^ k) for i in range(MP)])


def on_device(
    frames, intra_qkv, intra_out, intra_up, intra_down, inter_qkv, inter_out, inter_up, inter_down
):
    seq_count = lax.axis_size("seq")
    mine = lax.axis_index("mp").reshape(1)
    count = frames.shape[0]
    total = count * seq_count

    first = jnp.transpose(intra_qkv, (1, 2, 0)).reshape(-1, D)
    across = by(first, 2)
    first = [first, by(first, 1), across, by(across, 1)]
    rest = (
        jnp.transpose(inter_qkv, (1, 2, 0)).reshape(-1, D),
        inter_out,
        inter_up,
        inter_down,
        intra_out,
        intra_up,
        intra_down,
    )
    rest = pl.pallas_call(
        pack,
        out_shape=jax.ShapeDtypeStruct((1344, D), BF),
        in_specs=[IN_VMEM] * len(rest),
        out_specs=IN_VMEM,
        compiler_params=params(4),
        name="pack",
    )(*rest)
    rest, first[2] = lax.optimization_barrier((rest, across))
    rest = [rest, by(rest, 1), by(rest, 2)]

    rows, own_frames = pl.pallas_call(
        prepare,
        out_shape=(
            jax.ShapeDtypeStruct((count, 256, D), BF),
            jax.ShapeDtypeStruct((2, 32, count, D), BF),
        ),
        grid_spec=pltpu.PrefetchScalarGridSpec(
            num_scalar_prefetch=1,
            in_specs=[IN_VMEM],
            out_specs=[IN_VMEM] * 2,
            scratch_shapes=[pltpu.VMEM((16 * count, 16 * count), BF)],
        ),
        compiler_params=params(24),
        cost_estimate=pl.CostEstimate(flops=4 * 10**9, bytes_accessed=8 * 10**6, transcendentals=10**4),
        name="prepare",
    )(mine, jnp.transpose(frames, (1, 0, 2)))

    group = 4
    steps = count // group // 2
    attended = []
    for part in range(2):
        found = pl.pallas_call(
            intra_attention,
            out_shape=jax.ShapeDtypeStruct((count // 2, 64, D), BF),
            grid_spec=pltpu.PrefetchScalarGridSpec(
                num_scalar_prefetch=1,
                grid=(steps,),
                in_specs=[
                    pl.BlockSpec((group, 256, D), lambda i, *_, part=part: (i + steps * part, 0, 0))
                ]
                + [whole((192, D))] * 4,
                out_specs=pl.BlockSpec((group, 64, D), lambda i, *_: (i, 0, 0)),
                scratch_shapes=[pltpu.VMEM((3, D, D), BF)],
            ),
            compiler_params=params(20),
            cost_estimate=pl.CostEstimate(
                flops=5 * 10**9, bytes_accessed=2 * 10**6, transcendentals=15 * 10**5
            ),
            name="intra_attention",
        )(mine, rows, *first)
        if part == 0:
            rest[2], found = lax.optimization_barrier((rest[2], found))
            rest.append(by(rest[2], 1))
        attended.append(found)

    sent = pl.pallas_call(
        intra_feed_forward,
        out_shape=jax.ShapeDtypeStruct((seq_count, 2, count, D), BF),
        in_specs=[IN_VMEM] * 7,
        out_specs=IN_VMEM,
        compiler_params=params(24),
        cost_estimate=pl.CostEstimate(flops=3 * 10**9, bytes_accessed=3 * 10**6, transcendentals=0),
        name="intra_feed_forward",
    )(*attended, own_frames, *rest)
    sent = sent.reshape(seq_count, 2 * count, D)
    got = lax.all_to_all(sent, "seq", split_axis=0, concat_axis=0, tiled=True)
    summed = pl.pallas_call(
        inter_layer,
        out_shape=jax.ShapeDtypeStruct((total, D), BF),
        in_specs=[IN_VMEM] * 5,
        out_specs=IN_VMEM,
        scratch_shapes=attention_scratch(total),
        compiler_params=params(32),
        cost_estimate=pl.CostEstimate(flops=3 * 10**10, bytes_accessed=4 * 10**6, transcendentals=10**7),
        name="inter_layer",
    )(got.reshape(seq_count, 2, count, D), *rest)

    back = summed.reshape(seq_count, count, D)
    back = lax.all_to_all(back, "seq", split_axis=0, concat_axis=0, tiled=True)
    across = by(back, 2)
    pieces = [back, by(back, 1), across, by(across, 1)]
    return pl.pallas_call(
        assemble,
        out_shape=jax.ShapeDtypeStruct((HALF * count, D), BF),
        grid_spec=pltpu.PrefetchScalarGridSpec(
            num_scalar_prefetch=1,
            in_specs=[IN_VMEM] * 4,
            out_specs=IN_VMEM,
            scratch_shapes=[pltpu.VMEM((count, 128, D), BF)],
        ),
        compiler_params=params(12),
        cost_estimate=pl.CostEstimate(flops=10**9, bytes_accessed=4 * 10**6, transcendentals=0),
        name="assemble",
    )(mine, *pieces)


def solution(mesh):
    return jax.shard_map(
        on_device,
        mesh=mesh,
        in_specs=(
            P("seq", None, None),
            P(None, None, "mp"),
            P("mp", None),
            P(None, "mp"),
            P("mp", None),
            P(None, None, "mp"),
            P("mp", None),
            P(None, "mp"),
            P("mp", None),
        ),
        out_specs=P("seq", None),
        check_vma=False,
    )
```

```python
import functools

import jax
import jax.numpy as jnp
from jax import lax
from jax.experimental import pallas as pl
from jax.experimental.pallas import tpu as pltpu
from jax.sharding import PartitionSpec as P

HEADS = 8
HD = 32
K = 250
HALF = K // 2
D = 256
MP = 4
BF = jnp.bfloat16
F32 = jnp.float32
Q_SCALE = 1.4426950408889634 * HD ** (-0.5)
LOW = -1e30
IN_HBM = pl.BlockSpec(memory_space=pltpu.HBM)
IN_VMEM = pl.BlockSpec(memory_space=pltpu.VMEM)


def params(mebibytes):
    return pltpu.CompilerParams(vmem_limit_bytes=mebibytes * 1024 * 1024)


def dot(left, right, left_dim=1, right_dim=0):
    return lax.dot_general(
        left, right, (((left_dim,), (right_dim,)), ((), ())), preferred_element_type=F32
    )


def normed(values):
    centre = values - jnp.mean(values, axis=-1, keepdims=True)
    spread = jnp.mean(centre * centre, axis=-1, keepdims=True)
    return (centre * lax.rsqrt(spread + 1e-05)).astype(BF)


def put_attention_weights(shards, weights_ref):
    for k in range(MP):
        for t in range(weights_ref.shape[0]):
            weights_ref[t, 64 * k : 64 * k + 64, :] = shards[k][64 * t : 64 * t + 64, :]


def project(rows, weights_ref, query_ref, key_ref, value_ref):
    query_ref[...] = (dot(weights_ref[0], rows, 1, 1) * Q_SCALE).astype(BF)
    keys = dot(rows, weights_ref[1], 1, 1).astype(BF)
    lane = lax.broadcasted_iota(jnp.int32, (rows.shape[0], 128), 1) // HD
    for h in range(HEADS):
        part = keys[:, 128 * (h // 4) : 128 * (h // 4) + 128]
        key_ref[h] = jnp.where(lane == h % 4, part, jnp.zeros_like(part))
    values = dot(weights_ref[2], rows, 1, 1).astype(BF)
    for h in range(HEADS):
        value_ref[h, 0:HD, :] = values[HD * h : HD * h + HD, :]
        value_ref[h, HD:48, :] = jnp.ones((48 - HD, rows.shape[0]), BF)


def attend(columns, query_ref, key_ref, value_ref, attended_ref):
    def scores(h):
        at = 128 * (h // 4)
        return dot(key_ref[h], query_ref[at : at + 128, columns])

    following = scores(0)
    for h in range(HEADS):
        current = following
        if h + 1 < HEADS:
            following = scores(h + 1)
        top = jnp.max(current, axis=0, keepdims=True)
        weights = jnp.exp2(current - top).astype(BF)
        mixed = dot(value_ref[h], weights)
        attended_ref[HD * h : HD * h + HD, columns] = mixed[0:HD] * (1.0 / mixed[HD : HD + 1])


def swapped(outer, bits):
    inner = 1 << bits
    size = outer * inner
    to = lax.broadcasted_iota(jnp.int32, (size, size), 0)
    source = lax.broadcasted_iota(jnp.int32, (size, size), 1)
    return jnp.where((source & (inner - 1)) * outer + (source >> bits) == to, 1.0, 0.0).astype(BF)


def pack(*refs):
    sources, packed_ref, sems = refs[:-2], refs[-2], refs[-1]
    copies, at = [], 0
    for k, source in enumerate(sources):
        into = packed_ref.at[pl.ds(at, source.shape[0])]
        copies.append(pltpu.make_async_copy(source, into, sems.at[k]))
        copies[-1].start()
        at += source.shape[0]
    for copy in copies:
        copy.wait()


def prepare(mine_ref, frames_ref, n_ref, xq_ref, x_ref, turn_ref, sems):
    count = x_ref.shape[1]
    copies = []
    for k, (at, to) in enumerate(((0, 64), (64, HALF), (HALF, 189), (189, K))):
        part = pl.ds(at, to - at)
        copies.append(pltpu.make_async_copy(frames_ref.at[part], x_ref.at[part], sems.at[k]))
        copies[-1].start()
    turn_ref[...] = swapped(count, 4).T

    def put(to, x):
        rows = normed(x.astype(F32).reshape(16 * count, D))
        rows = dot(turn_ref[...], rows).astype(BF)
        for u in range(count):
            n_ref[u, pl.ds(to, 16), :] = rows[16 * u : 16 * u + 16]

    def early(b, carry):
        at = pl.multiple_of(b * 16, 16)
        put(at, x_ref[pl.ds(at, 16)])
        return carry

    def late(b, carry):
        at = pl.multiple_of(b * 16, 16)
        put(128 + at, x_ref[pl.ds(HALF + at, 16)])
        return carry

    copies[0].wait()
    lax.fori_loop(0, 4, early, 0, unroll=True)
    copies[1].wait()
    copies[2].wait()
    lax.fori_loop(4, 8, early, 0, unroll=True)
    lax.fori_loop(0, 4, late, 0, unroll=True)
    copies[3].wait()
    lax.fori_loop(4, 7, late, 0, unroll=True)
    put(240, jnp.concatenate([x_ref[HALF + 112 : K], x_ref[K - 3 : K]], axis=0))

    def residual(j, carry):
        r = mine_ref[0] * 32 + j
        xq_ref[0, j] = x_ref[r]
        xq_ref[1, j] = x_ref[jnp.minimum(HALF + r, K - 1)]
        return carry

    lax.fori_loop(0, 32, residual, 0)


def intra_attention(mine_ref, n_ref, w0, w1, w2, w3, o_ref, weights_ref):
    @pl.when(pl.program_id(0) == 0)
    def _():
        put_attention_weights((w0, w1, w2, w3), weights_ref)

    own = pl.multiple_of(mine_ref[0] * 32, 32)
    count = n_ref.shape[0]
    row = lax.broadcasted_iota(jnp.int32, (256, 256), 0)
    lane = lax.broadcasted_iota(jnp.int32, (256, 256), 1)
    valid = (row % 128) < HALF
    same = (row % 128) // HD == lane // 64
    keys, queries, values = [], [], []
    for u in range(count):
        rows = n_ref[u]
        few = jnp.concatenate(
            [n_ref[u, pl.ds(own, 32), :], n_ref[u, pl.ds(128 + own, 32), :]], axis=0
        )
        keys.append(dot(rows, weights_ref[1], 1, 1).astype(BF))
        query = dot(weights_ref[0], jnp.concatenate([few] * 4, axis=0), 1, 1) * Q_SCALE
        queries.append(jnp.where(same, query, 0.0).astype(BF))
        values.append(dot(weights_ref[2], rows, 1, 1).astype(BF))
    parts = [(u, g) for u in range(count) for g in range(2)]

    def scores(u, g):
        part = slice(128 * g, 128 * g + 128)
        return jnp.where(valid, dot(keys[u][:, part], queries[u][part]), LOW)

    following = scores(*parts[0])
    found = []
    ones = jnp.ones((16, 256), BF)
    for at, (u, g) in enumerate(parts):
        current = following
        if at + 1 < len(parts):
            following = scores(*parts[at + 1])
        top = jnp.max(current, axis=0, keepdims=True)
        weights = jnp.exp2(current - top).astype(BF)
        mixed = dot(jnp.concatenate([values[u][128 * g : 128 * g + 128], ones], axis=0), weights)
        mixed = jnp.where(same[0:128], mixed[0:128] * (1.0 / mixed[128:129]), 0.0)
        mixed = (mixed[:, 0:128] + mixed[:, 128:256]).T
        found.append((mixed[0:64] + mixed[64:128]).astype(BF))
    for u in range(count):
        o_ref[u] = jnp.concatenate(found[2 * u : 2 * u + 2], axis=1)


def feed_forward(middle, up, down):
    middle = middle.astype(F32)
    rows = normed(middle)
    total = middle
    for u, d in zip(up, down):
        hidden = jnp.maximum(dot(rows, u), 0.0).astype(BF)
        total = total + dot(hidden, d)
    return total.astype(BF)


def intra_feed_forward(a0_ref, a1_ref, xq_ref, w0, w1, w2, w3, o_ref):
    shards = (w0, w1, w2, w3)
    count = xq_ref.shape[2]
    out = jnp.concatenate([w[768:832, :] for w in shards], axis=0)
    up = [w[832:1088, :] for w in shards]
    down = [w[1088:1344, :] for w in shards]
    turn = swapped(count, 3)
    for half in range(2):
        for pair in range(2):
            rows = []
            for at in (32 * half + 16 * pair, 32 * half + 16 * pair + 8):
                taken = [
                    ref[u, at : at + 8, :].astype(F32)
                    for ref in (a0_ref, a1_ref)
                    for u in range(ref.shape[0])
                ]
                rows.append(dot(turn, jnp.concatenate(taken, axis=0).astype(BF)).astype(BF))
            attended = jnp.concatenate(rows, axis=0)
            part = slice(16 * pair, 16 * pair + 16)
            x = xq_ref[half, part].astype(F32).reshape(16 * count, D)
            middle = (x + dot(attended, out)).astype(BF)
            done = feed_forward(middle, up, down).astype(F32)
            o_ref[part, half] = done.reshape(16, count, D).astype(BF)


def inter_layer(x_ref, w0, w1, w2, w3, o_ref, weights_ref, query_ref, key_ref, value_ref, attended_ref, later_ref):
    shards = (w0, w1, w2, w3)
    put_attention_weights(shards, weights_ref)
    for half in (1, 0):
        x = x_ref[:, half].astype(F32).reshape(later_ref.shape)
        project(normed(x), weights_ref, query_ref, key_ref, value_ref)

        def block(i, carry):
            columns = pl.ds(pl.multiple_of(i * 256, 256), 256)
            attend(columns, query_ref, key_ref, value_ref, attended_ref)
            return carry

        lax.fori_loop(0, x.shape[0] // 256, block, 0)
        attended = attended_ref[...].T.astype(BF)
        middle = (x + dot(attended, weights_ref[3])).astype(BF)
        done = feed_forward(
            middle, [w[256:512, :] for w in shards], [w[512:768, :] for w in shards]
        )
        if half == 1:
            first = lax.broadcasted_iota(jnp.int32, done.shape, 0) == 0
            later_ref[...] = jnp.where(first, 0.0, pltpu.roll(done.astype(F32), 1, 0))
        else:
            summed = (done.astype(F32) + later_ref[...]).reshape(x_ref.shape[0], *x_ref.shape[2:])
            for copy in range(2):
                o_ref[:, copy] = summed.astype(BF)


def assemble(mine_ref, p0, p1, o_ref, rows_ref):
    turn = swapped(32, 3)
    for piece, core, z in ((p, core, z) for core, p in enumerate((p0, p1)) for z in range(2)):
        at = pl.multiple_of((2 * z + ((mine_ref[0] & 1) ^ core)) * 32, 32)
        for part in range(3):
            taken = [piece[2 * s + z, 8 * part : 8 * part + 8, :].astype(F32) for s in range(32)]
            rows = dot(turn, jnp.concatenate(taken, axis=0).astype(BF)).astype(BF)
            for u in range(8):
                rows_ref[8 * part + u, pl.ds(at, 32), :] = rows[32 * u : 32 * u + 32]
    to = lax.broadcasted_iota(jnp.int32, (128, 256), 0)
    source = lax.broadcasted_iota(jnp.int32, (128, 256), 1)
    for b in range(24):
        place = to + 3 * b
        place = jnp.where(place < HALF, place, place + 3)
        pick = jnp.where(place == source, 1.0, 0.0).astype(BF)
        rows = jnp.concatenate([rows_ref[b], rows_ref[min(b + 1, 23)]], axis=0)
        size = min(128, 3000 - 128 * b)
        o_ref[128 * b : 128 * b + size, :] = dot(pick, rows)[0:size].astype(BF)


def whole(shape):
    return pl.BlockSpec(shape, lambda i, *_: (0,) * len(shape))


def attention_scratch(length):
    return [
        pltpu.VMEM((4, D, D), BF),
        pltpu.VMEM((D, length), BF),
        pltpu.VMEM((HEADS, length, 128), BF),
        pltpu.VMEM((HEADS, 48, length), BF),
        pltpu.VMEM((D, length), F32),
    ]


def by(shard, k):
    return lax.ppermute(shard, "mp", [(i, i ^ k) for i in range(MP)])


def on_device(
    frames, intra_qkv, intra_out, intra_up, intra_down, inter_qkv, inter_out, inter_up, inter_down
):
    seq_count = lax.axis_size("seq")
    mine = lax.axis_index("mp").reshape(1)
    count = frames.shape[0]
    total = count * seq_count

    first = jnp.transpose(intra_qkv, (1, 2, 0)).reshape(-1, D)
    across = by(first, 2)
    first = [first, by(first, 1), across, by(across, 1)]
    rest = (
        jnp.transpose(inter_qkv, (1, 2, 0)).reshape(-1, D),
        inter_out,
        inter_up,
        inter_down,
        intra_out,
        intra_up,
        intra_down,
    )
    rest = pl.pallas_call(
        pack,
        out_shape=jax.ShapeDtypeStruct((1344, D), BF),
        in_specs=[IN_HBM] * len(rest),
        out_specs=IN_VMEM,
        scratch_shapes=[pltpu.SemaphoreType.DMA((len(rest),))],
        compiler_params=params(4),
        name="pack",
    )(*[pltpu.with_memory_space_constraint(a, pltpu.HBM) for a in rest])
    rest, first[2] = lax.optimization_barrier((rest, across))
    rest = [rest, by(rest, 1), by(rest, 2)]

    rows, own_frames = pl.pallas_call(
        prepare,
        out_shape=(
            jax.ShapeDtypeStruct((count, 256, D), BF),
            jax.ShapeDtypeStruct((2, 32, count, D), BF),
        ),
        grid_spec=pltpu.PrefetchScalarGridSpec(
            num_scalar_prefetch=1,
            in_specs=[IN_HBM],
            out_specs=[IN_VMEM] * 2,
            scratch_shapes=[
                pltpu.VMEM((K, count, D), BF),
                pltpu.VMEM((16 * count, 16 * count), BF),
                pltpu.SemaphoreType.DMA((4,)),
            ],
        ),
        compiler_params=params(24),
        cost_estimate=pl.CostEstimate(flops=4 * 10**9, bytes_accessed=8 * 10**6, transcendentals=10**4),
        name="prepare",
    )(mine, pltpu.with_memory_space_constraint(jnp.transpose(frames, (1, 0, 2)), pltpu.HBM))

    group = 4
    attended = []
    for start, steps in ((0, 4), (4, 2)):
        found = pl.pallas_call(
            intra_attention,
            out_shape=jax.ShapeDtypeStruct((group * steps, 64, D), BF),
            grid_spec=pltpu.PrefetchScalarGridSpec(
                num_scalar_prefetch=1,
                grid=(steps,),
                in_specs=[
                    pl.BlockSpec((group, 256, D), lambda i, *_, start=start: (i + start, 0, 0))
                ]
                + [whole((192, D))] * 4,
                out_specs=pl.BlockSpec((group, 64, D), lambda i, *_: (i, 0, 0)),
                scratch_shapes=[pltpu.VMEM((3, D, D), BF)],
            ),
            compiler_params=params(20),
            cost_estimate=pl.CostEstimate(
                flops=5 * 10**9, bytes_accessed=2 * 10**6, transcendentals=15 * 10**5
            ),
            name="intra_attention",
        )(mine, rows, *first)
        if start == 0:
            rest[2], found = lax.optimization_barrier((rest[2], found))
            rest.append(by(rest[2], 1))
        attended.append(found)

    sent = pl.pallas_call(
        intra_feed_forward,
        out_shape=jax.ShapeDtypeStruct((seq_count, 2, count, D), BF),
        in_specs=[IN_VMEM] * 7,
        out_specs=IN_VMEM,
        compiler_params=params(24),
        cost_estimate=pl.CostEstimate(flops=3 * 10**9, bytes_accessed=3 * 10**6, transcendentals=0),
        name="intra_feed_forward",
    )(*attended, own_frames, *rest)
    sent = sent.reshape(seq_count, 2 * count, D)
    got = lax.all_to_all(sent, "seq", split_axis=0, concat_axis=0, tiled=True)
    summed = pl.pallas_call(
        inter_layer,
        out_shape=jax.ShapeDtypeStruct((seq_count, 2, count, D), BF),
        in_specs=[IN_VMEM] * 5,
        out_specs=IN_VMEM,
        scratch_shapes=attention_scratch(total) + [pltpu.VMEM((total, D), F32)],
        compiler_params=params(32),
        cost_estimate=pl.CostEstimate(flops=3 * 10**10, bytes_accessed=4 * 10**6, transcendentals=10**7),
        name="inter_layer",
    )(got.reshape(seq_count, 2, count, D), *rest)

    back = summed.reshape(2 * seq_count, count, D)
    chips = [(s, z) for s in range(seq_count) for z in range(2)]
    groups = [[MP * s + 2 * z + core for s, z in chips] for core in range(2)]
    back = lax.all_to_all(
        back, ("seq", "mp"), split_axis=0, concat_axis=0, tiled=True, axis_index_groups=groups
    )
    pieces = [back, by(back, 1)]
    return pl.pallas_call(
        assemble,
        out_shape=jax.ShapeDtypeStruct((HALF * count, D), BF),
        grid_spec=pltpu.PrefetchScalarGridSpec(
            num_scalar_prefetch=1,
            in_specs=[IN_VMEM] * 2,
            out_specs=IN_VMEM,
            scratch_shapes=[pltpu.VMEM((count, 128, D), BF)],
        ),
        compiler_params=params(12),
        cost_estimate=pl.CostEstimate(flops=10**9, bytes_accessed=4 * 10**6, transcendentals=0),
        name="assemble",
    )(mine, *pieces)


def solution(mesh):
    return jax.shard_map(
        on_device,
        mesh=mesh,
        in_specs=(
            P("seq", None, None),
            P(None, None, "mp"),
            P("mp", None),
            P(None, "mp"),
            P("mp", None),
            P(None, None, "mp"),
            P("mp", None),
            P(None, "mp"),
            P("mp", None),
        ),
        out_specs=P("seq", None),
        check_vma=False,
    )
```

```python
import functools

import jax
import jax.numpy as jnp
from jax import lax
from jax.experimental import pallas as pl
from jax.experimental.pallas import tpu as pltpu
from jax.sharding import PartitionSpec as P

HEADS = 8
HD = 32
K = 250
HALF = K // 2
D = 256
MP = 4
BF = jnp.bfloat16
F32 = jnp.float32
Q_SCALE = 1.4426950408889634 * HD ** (-0.5)
LOW = -1e30
IN_HBM = pl.BlockSpec(memory_space=pltpu.HBM)
IN_VMEM = pl.BlockSpec(memory_space=pltpu.VMEM)


def params(mebibytes):
    return pltpu.CompilerParams(vmem_limit_bytes=mebibytes * 1024 * 1024)


def dot(left, right, left_dim=1, right_dim=0):
    return lax.dot_general(
        left, right, (((left_dim,), (right_dim,)), ((), ())), preferred_element_type=F32
    )


def normed(values):
    centre = values - jnp.mean(values, axis=-1, keepdims=True)
    spread = jnp.mean(centre * centre, axis=-1, keepdims=True)
    return (centre * lax.rsqrt(spread + 1e-05)).astype(BF)


def put_attention_weights(shards, weights_ref):
    for k in range(MP):
        for t in range(weights_ref.shape[0]):
            weights_ref[t, 64 * k : 64 * k + 64, :] = shards[k][64 * t : 64 * t + 64, :]


def project(rows, weights_ref, query_ref, key_ref, value_ref):
    query_ref[...] = (dot(weights_ref[0], rows, 1, 1) * Q_SCALE).astype(BF)
    keys = dot(rows, weights_ref[1], 1, 1).astype(BF)
    lane = lax.broadcasted_iota(jnp.int32, (rows.shape[0], 128), 1) // HD
    for h in range(HEADS):
        part = keys[:, 128 * (h // 4) : 128 * (h // 4) + 128]
        key_ref[h] = jnp.where(lane == h % 4, part, jnp.zeros_like(part))
    values = dot(weights_ref[2], rows, 1, 1).astype(BF)
    for h in range(HEADS):
        value_ref[h, 0:HD, :] = values[HD * h : HD * h + HD, :]
        value_ref[h, HD:48, :] = jnp.ones((48 - HD, rows.shape[0]), BF)


def attend(query_ref, key_ref, value_ref, attended_ref):
    def scores(h):
        half = 128 * (h // 4)
        return dot(key_ref[h], query_ref[half : half + 128, :])

    following = scores(0)
    for h in range(HEADS):
        current = following
        if h + 1 < HEADS:
            following = scores(h + 1)
        top = jnp.max(current, axis=0, keepdims=True)
        weights = jnp.exp2(current - top).astype(BF)
        mixed = dot(value_ref[h], weights)
        attended_ref[HD * h : HD * h + HD, :] = mixed[0:HD] * (1.0 / mixed[HD : HD + 1])


def swapped(outer, bits):
    inner = 1 << bits
    size = outer * inner
    to = lax.broadcasted_iota(jnp.int32, (size, size), 0)
    source = lax.broadcasted_iota(jnp.int32, (size, size), 1)
    return jnp.where((source & (inner - 1)) * outer + (source >> bits) == to, 1.0, 0.0).astype(BF)


def pack(early, *refs):
    sources, (first_ref, rest_ref, sems) = refs[:-3], refs[-3:]
    copies = []
    for some, into in ((range(early), first_ref), (range(early, len(sources)), rest_ref)):
        at = 0
        for k in some:
            size = sources[k].shape[0]
            copies.append(pltpu.make_async_copy(sources[k], into.at[pl.ds(at, size)], sems.at[k]))
            copies[-1].start()
            at += size
    for copy in copies:
        copy.wait()


def prepare(half, mine_ref, frames_ref, n_ref, xq_ref, x_ref, turn_ref, sems):
    count = x_ref.shape[1]
    length = 128 if half == 0 else K - HALF
    copies = []
    for k, (at, to) in enumerate(((0, 64), (64, length))):
        copies.append(
            pltpu.make_async_copy(
                frames_ref.at[pl.ds(half * HALF + at, to - at)],
                x_ref.at[pl.ds(at, to - at)],
                sems.at[k],
            )
        )
        copies[-1].start()
    to = lax.broadcasted_iota(jnp.int32, turn_ref.shape, 0)
    source = lax.broadcasted_iota(jnp.int32, turn_ref.shape, 1)
    turn_ref[...] = jnp.where((to & 15) * count + (to >> 4) == source, 1.0, 0.0).astype(BF)
    for b in range(8):
        if b == 0:
            copies[0].wait()
        if b == 4:
            copies[1].wait()
            if length < 128:
                x_ref[length:128] = x_ref[length - (128 - length) : length]
        rows = normed(x_ref[16 * b : 16 * b + 16].astype(F32).reshape(16 * count, D))
        rows = dot(turn_ref[...], rows).astype(BF)
        for u in range(count):
            n_ref[u, 16 * b : 16 * b + 16, :] = rows[16 * u : 16 * u + 16]
    xq_ref[...] = x_ref[pl.ds(mine_ref[0] * 32, 32)]


def intra_attention(mine_ref, early_ref, late_ref, w0, w1, w2, w3, o_ref, weights_ref):
    @pl.when(pl.program_id(0) == 0)
    def _():
        put_attention_weights((w0, w1, w2, w3), weights_ref)

    own = pl.multiple_of(mine_ref[0] * 32, 32)
    count = early_ref.shape[0]
    row = lax.broadcasted_iota(jnp.int32, (256, 256), 0)
    lane = lax.broadcasted_iota(jnp.int32, (256, 256), 1)
    same = (row & 127) >> 5 == lane >> 6
    valid = jnp.concatenate([row[0:8] < 5] * 2, axis=1)
    rows, few = [], []
    for u in range(count):
        rows += [early_ref[u], late_ref[u]]
        few += [early_ref[u, pl.ds(own, 32), :], late_ref[u, pl.ds(own, 32), :]] * 4
    rows = jnp.concatenate(rows, axis=0)
    keys = dot(rows, weights_ref[1], 1, 1).astype(BF)
    query = dot(weights_ref[0], jnp.concatenate(few, axis=0), 1, 1) * Q_SCALE
    values = dot(weights_ref[2], rows, 1, 1).astype(BF)
    ones = jnp.ones((16, 256), BF)

    def scores(u):
        at = slice(256 * u, 256 * u + 256)
        own_query = query[:, at]
        low = jnp.where(same & (row < 128), own_query, 0.0)
        high = jnp.where(same & (row >= 128), own_query, 0.0)
        score = dot(keys[at], jnp.concatenate([low, high], axis=1).astype(BF))
        pieces = []
        for at in (0, 128):
            pieces += [score[at : at + 120], jnp.where(valid, score[at + 120 : at + 128], LOW)]
        return jnp.concatenate(pieces, axis=0)

    following = scores(0)
    found = []
    for u in range(count):
        current = following
        if u + 1 < count:
            following = scores(u + 1)
        top = jnp.max(current, axis=0, keepdims=True)
        weights = jnp.exp2(current - top).astype(BF)
        for g in range(2):
            value = values[128 * g : 128 * g + 128, 256 * u : 256 * u + 256]
            mixed = dot(
                jnp.concatenate([value, ones], axis=0), weights[:, 256 * g : 256 * g + 256]
            )
            mixed = jnp.where(same[0:128], mixed[0:128] * (1.0 / mixed[128:129]), 0.0)
            mixed = (mixed[:, 0:128] + mixed[:, 128:256]).T
            found.append((mixed[0:64] + mixed[64:128]).astype(BF))
    for u in range(count):
        o_ref[u] = jnp.concatenate(found[2 * u : 2 * u + 2], axis=1)


def add_hidden(rows, total, up, down):
    hidden = jnp.maximum(dot(rows, up[0]), 0.0).astype(BF)
    for k in range(len(up)):
        ready = hidden
        if k + 1 < len(up):
            hidden = jnp.maximum(dot(rows, up[k + 1]), 0.0).astype(BF)
        total = total + dot(ready, down[k])
    return total


def feed_forward(middles, up, down):
    done = []
    following = normed(middles[0].astype(F32))
    for at, middle in enumerate(middles):
        rows = following
        if at + 1 < len(middles):
            following = normed(middles[at + 1].astype(F32))
        done.append((rows, add_hidden(rows, middle.astype(F32), up, down)))
    return done


def intra_feed_forward(a_ref, xq0_ref, xq1_ref, f0, f1, f2, f3, w0, w1, w2, rows_ref, total_ref):
    shards = (w0, w1, w2)
    count = xq0_ref.shape[1]
    out = jnp.concatenate([w[192:256, :] for w in (f0, f1, f2, f3)], axis=0)
    up = [w[768:1024, :] for w in shards]
    down = [w[1024:1280, :] for w in shards]
    turn = swapped(count, 3)
    middles = []
    for half in range(2):
        for pair in range(2):
            rows = []
            for at in (32 * half + 16 * pair, 32 * half + 16 * pair + 8):
                taken = [a_ref[u, at : at + 8, :].astype(F32) for u in range(count)]
                rows.append(dot(turn, jnp.concatenate(taken, axis=0).astype(BF)).astype(BF))
            x = (xq0_ref, xq1_ref)[half][16 * pair : 16 * pair + 16].astype(F32).reshape(16 * count, D)
            middles.append((x + dot(jnp.concatenate(rows, axis=0), out)).astype(BF))
    size = 16 * count
    for at, (rows, total) in enumerate(feed_forward(middles, up, down)):
        rows_ref[size * at : size * at + size, :] = rows
        total_ref[size * at : size * at + size, :] = total


def intra_last_hidden(rows_ref, total_ref, w3, o_ref):
    count = o_ref.shape[2]
    size = 16 * count
    for half in range(2):
        for pair in range(2):
            at = slice(size * (2 * half + pair), size * (2 * half + pair + 1))
            total = add_hidden(rows_ref[at], total_ref[at], [w3[768:1024, :]], [w3[1024:1280, :]])
            total = total.astype(BF).astype(F32).reshape(16, count, D)
            o_ref[16 * pair : 16 * pair + 16, half] = total.astype(BF)


def inter_layer(x_ref, w0, w1, w2, w3, o_ref, weights_ref, query_ref, key_ref, value_ref, attended_ref, later_ref):
    shards = (w0, w1, w2, w3)
    put_attention_weights(shards, weights_ref)
    for half in (1, 0):
        x = x_ref[:, half].astype(F32).reshape(later_ref.shape)
        project(normed(x), weights_ref, query_ref, key_ref, value_ref)
        attend(query_ref, key_ref, value_ref, attended_ref)
        attended = attended_ref[...].T.astype(BF)
        middle = (x + dot(attended, weights_ref[3])).astype(BF)
        done = feed_forward(
            [middle[at : at + 256] for at in range(0, x.shape[0], 256)],
            [w[256:512, :] for w in shards],
            [w[512:768, :] for w in shards],
        )
        done = jnp.concatenate([total.astype(BF) for _, total in done], axis=0)
        if half == 1:
            first = lax.broadcasted_iota(jnp.int32, done.shape, 0) == 0
            later_ref[...] = jnp.where(first, 0.0, pltpu.roll(done.astype(F32), 1, 0))
        else:
            summed = (done.astype(F32) + later_ref[...]).reshape(x_ref.shape[0], *x_ref.shape[2:])
            for copy in range(2):
                o_ref[:, copy] = summed.astype(BF)


def assemble(mine_ref, p0, p1, o_ref, rows_ref):
    turn = swapped(32, 3)
    for piece, core, z in ((p, core, z) for core, p in enumerate((p0, p1)) for z in range(2)):
        at = pl.multiple_of((2 * z + ((mine_ref[0] & 1) ^ core)) * 32, 32)
        for part in range(3):
            taken = [piece[2 * s + z, 8 * part : 8 * part + 8, :].astype(F32) for s in range(32)]
            rows = dot(turn, jnp.concatenate(taken, axis=0).astype(BF)).astype(BF)
            for u in range(8):
                rows_ref[8 * part + u, pl.ds(at, 32), :] = rows[32 * u : 32 * u + 32]
    to = lax.broadcasted_iota(jnp.int32, (128, 256), 0)
    source = lax.broadcasted_iota(jnp.int32, (128, 256), 1)
    for b in range(24):
        place = to + 3 * b
        place = jnp.where(place < HALF, place, place + 3)
        pick = jnp.where(place == source, 1.0, 0.0).astype(BF)
        rows = jnp.concatenate([rows_ref[b], rows_ref[min(b + 1, 23)]], axis=0)
        size = min(128, 3000 - 128 * b)
        o_ref[128 * b : 128 * b + size, :] = dot(pick, rows)[0:size].astype(BF)


def whole(shape):
    return pl.BlockSpec(shape, lambda i, *_: (0,) * len(shape))


def attention_scratch(length):
    return [
        pltpu.VMEM((4, D, D), BF),
        pltpu.VMEM((D, length), BF),
        pltpu.VMEM((HEADS, length, 128), BF),
        pltpu.VMEM((HEADS, 48, length), BF),
        pltpu.VMEM((D, length), F32),
    ]


def by(shard, k):
    return lax.ppermute(shard, "mp", [(i, i ^ k) for i in range(MP)])


def on_device(
    frames, intra_qkv, intra_out, intra_up, intra_down, inter_qkv, inter_out, inter_up, inter_down
):
    seq_count = lax.axis_size("seq")
    mine = lax.axis_index("mp").reshape(1)
    count = frames.shape[0]
    total = count * seq_count

    weights = (
        jnp.transpose(intra_qkv, (1, 2, 0)).reshape(-1, D),
        intra_out,
        jnp.transpose(inter_qkv, (1, 2, 0)).reshape(-1, D),
        inter_out,
        inter_up,
        inter_down,
        intra_up,
        intra_down,
    )
    first, rest = pl.pallas_call(
        functools.partial(pack, 2),
        out_shape=(jax.ShapeDtypeStruct((256, D), BF), jax.ShapeDtypeStruct((1280, D), BF)),
        in_specs=[IN_HBM] * len(weights),
        out_specs=[IN_VMEM] * 2,
        scratch_shapes=[pltpu.SemaphoreType.DMA((len(weights),))],
        compiler_params=params(4),
        name="pack",
    )(*[pltpu.with_memory_space_constraint(a, pltpu.HBM) for a in weights])
    across = by(first, 2)
    first = [first, by(first, 1), across, by(across, 1)]

    rows, own_frames = [], []
    stored = pltpu.with_memory_space_constraint(jnp.transpose(frames, (1, 0, 2)), pltpu.HBM)
    for half in range(2):
        found = pl.pallas_call(
            functools.partial(prepare, half),
            out_shape=(
                jax.ShapeDtypeStruct((count, 128, D), BF),
                jax.ShapeDtypeStruct((32, count, D), BF),
            ),
            grid_spec=pltpu.PrefetchScalarGridSpec(
                num_scalar_prefetch=1,
                in_specs=[IN_HBM],
                out_specs=[IN_VMEM] * 2,
                scratch_shapes=[
                    pltpu.VMEM((128, count, D), BF),
                    pltpu.VMEM((16 * count, 16 * count), BF),
                    pltpu.SemaphoreType.DMA((2,)),
                ],
            ),
            compiler_params=params(16),
            cost_estimate=pl.CostEstimate(flops=10**9, bytes_accessed=4 * 10**6, transcendentals=10**4),
            name="prepare",
        )(mine, stored)
        rows.append(found[0])
        own_frames.append(found[1])
        if half == 0:
            rest, first[2], rows[0] = lax.optimization_barrier((rest, across, rows[0]))
            rest = [rest, by(rest, 1), by(rest, 2)]

    group = 8
    attended = pl.pallas_call(
        intra_attention,
        out_shape=jax.ShapeDtypeStruct((count, 64, D), BF),
        grid_spec=pltpu.PrefetchScalarGridSpec(
            num_scalar_prefetch=1,
            grid=(count // group,),
            in_specs=[pl.BlockSpec((group, 128, D), lambda i, *_: (i, 0, 0))] * 2
            + [whole((192, D))] * 4,
            out_specs=pl.BlockSpec((group, 64, D), lambda i, *_: (i, 0, 0)),
            scratch_shapes=[pltpu.VMEM((3, D, D), BF)],
        ),
        compiler_params=params(20),
        cost_estimate=pl.CostEstimate(flops=2 * 10**9, bytes_accessed=4 * 10**6, transcendentals=3 * 10**6),
        name="intra_attention",
    )(mine, *rows, *first)
    rest[2], attended = lax.optimization_barrier((rest[2], attended))
    rest.append(by(rest[2], 1))

    normed_rows, partial_sums = pl.pallas_call(
        intra_feed_forward,
        out_shape=(
            jax.ShapeDtypeStruct((64 * count, D), BF),
            jax.ShapeDtypeStruct((64 * count, D), F32),
        ),
        in_specs=[IN_VMEM] * 10,
        out_specs=[IN_VMEM] * 2,
        compiler_params=params(24),
        cost_estimate=pl.CostEstimate(flops=3 * 10**9, bytes_accessed=3 * 10**6, transcendentals=0),
        name="intra_feed_forward",
    )(attended, *own_frames, *first, *rest[:3])
    sent = pl.pallas_call(
        intra_last_hidden,
        out_shape=jax.ShapeDtypeStruct((seq_count, 2, count, D), BF),
        in_specs=[IN_VMEM] * 3,
        out_specs=IN_VMEM,
        compiler_params=params(16),
        cost_estimate=pl.CostEstimate(flops=10**9, bytes_accessed=3 * 10**6, transcendentals=0),
        name="intra_last_hidden",
    )(normed_rows, partial_sums, rest[3])
    sent = sent.reshape(seq_count, 2 * count, D)
    got = lax.all_to_all(sent, "seq", split_axis=0, concat_axis=0, tiled=True)
    summed = pl.pallas_call(
        inter_layer,
        out_shape=jax.ShapeDtypeStruct((seq_count, 2, count, D), BF),
        in_specs=[IN_VMEM] * 5,
        out_specs=IN_VMEM,
        scratch_shapes=attention_scratch(total) + [pltpu.VMEM((total, D), F32)],
        compiler_params=params(32),
        cost_estimate=pl.CostEstimate(flops=3 * 10**10, bytes_accessed=4 * 10**6, transcendentals=10**7),
        name="inter_layer",
    )(got.reshape(seq_count, 2, count, D), *rest)

    back = summed.reshape(2 * seq_count, count, D)
    chips = [(s, z) for s in range(seq_count) for z in range(2)]
    groups = [[MP * s + 2 * z + core for s, z in chips] for core in range(2)]
    back = lax.all_to_all(
        back, ("seq", "mp"), split_axis=0, concat_axis=0, tiled=True, axis_index_groups=groups
    )
    pieces = [back, by(back, 1)]
    return pl.pallas_call(
        assemble,
        out_shape=jax.ShapeDtypeStruct((HALF * count, D), BF),
        grid_spec=pltpu.PrefetchScalarGridSpec(
            num_scalar_prefetch=1,
            in_specs=[IN_VMEM] * 2,
            out_specs=IN_VMEM,
            scratch_shapes=[pltpu.VMEM((count, 128, D), BF)],
        ),
        compiler_params=params(12),
        cost_estimate=pl.CostEstimate(flops=10**9, bytes_accessed=4 * 10**6, transcendentals=0),
        name="assemble",
    )(mine, *pieces)


def solution(mesh):
    return jax.shard_map(
        on_device,
        mesh=mesh,
        in_specs=(
            P("seq", None, None),
            P(None, None, "mp"),
            P("mp", None),
            P(None, "mp"),
            P("mp", None),
            P(None, None, "mp"),
            P("mp", None),
            P(None, "mp"),
            P("mp", None),
        ),
        out_specs=P("seq", None),
        check_vma=False,
    )
```

```python
import functools

import jax
import jax.numpy as jnp
from jax import lax
from jax.experimental import pallas as pl
from jax.experimental.pallas import tpu as pltpu
from jax.sharding import PartitionSpec as P

HEADS = 8
HD = 32
K = 250
HALF = K // 2
D = 256
MP = 4
BF = jnp.bfloat16
F32 = jnp.float32
Q_SCALE = 1.4426950408889634 * HD ** (-0.5)
LOW = -1e30
IN_HBM = pl.BlockSpec(memory_space=pltpu.HBM)
IN_VMEM = pl.BlockSpec(memory_space=pltpu.VMEM)


def params(mebibytes):
    return pltpu.CompilerParams(vmem_limit_bytes=mebibytes * 1024 * 1024)


def dot(left, right, left_dim=1, right_dim=0):
    return lax.dot_general(
        left, right, (((left_dim,), (right_dim,)), ((), ())), preferred_element_type=F32
    )


def normed(values):
    centre = values - jnp.mean(values, axis=-1, keepdims=True)
    spread = jnp.mean(centre * centre, axis=-1, keepdims=True)
    return (centre * lax.rsqrt(spread + 1e-05)).astype(BF)


def put_attention_weights(shards, weights_ref):
    for k in range(MP):
        for t in range(weights_ref.shape[0]):
            weights_ref[t, 64 * k : 64 * k + 64, :] = shards[k][64 * t : 64 * t + 64, :]


def project(rows, weights_ref, query_ref, key_ref, value_ref):
    query_ref[...] = (dot(weights_ref[0], rows, 1, 1) * Q_SCALE).astype(BF)
    keys = dot(rows, weights_ref[1], 1, 1).astype(BF)
    lane = lax.broadcasted_iota(jnp.int32, (rows.shape[0], 128), 1) // HD
    for h in range(HEADS):
        part = keys[:, 128 * (h // 4) : 128 * (h // 4) + 128]
        key_ref[h] = jnp.where(lane == h % 4, part, jnp.zeros_like(part))
    values = dot(weights_ref[2], rows, 1, 1).astype(BF)
    for h in range(HEADS):
        value_ref[h, 0:HD, :] = values[HD * h : HD * h + HD, :]
        value_ref[h, HD:48, :] = jnp.ones((48 - HD, rows.shape[0]), BF)


def attend(query_ref, key_ref, value_ref, attended_ref):
    def scores(h):
        half = 128 * (h // 4)
        return dot(key_ref[h], query_ref[half : half + 128, :])

    following = scores(0)
    for h in range(HEADS):
        current = following
        if h + 1 < HEADS:
            following = scores(h + 1)
        top = jnp.max(current, axis=0, keepdims=True)
        weights = jnp.exp2(current - top).astype(BF)
        mixed = dot(value_ref[h], weights)
        attended_ref[HD * h : HD * h + HD, :] = mixed[0:HD] * (1.0 / mixed[HD : HD + 1])


def swapped(outer, bits):
    inner = 1 << bits
    size = outer * inner
    to = lax.broadcasted_iota(jnp.int32, (size, size), 0)
    source = lax.broadcasted_iota(jnp.int32, (size, size), 1)
    return jnp.where((source & (inner - 1)) * outer + (source >> bits) == to, 1.0, 0.0).astype(BF)


def pack(early, *refs):
    sources, (first_ref, rest_ref, sems) = refs[:-3], refs[-3:]
    copies = []
    for some, into in ((range(early), first_ref), (range(early, len(sources)), rest_ref)):
        at = 0
        for k in some:
            size = sources[k].shape[0]
            copies.append(pltpu.make_async_copy(sources[k], into.at[pl.ds(at, size)], sems.at[k]))
            copies[-1].start()
            at += size
    for copy in copies:
        copy.wait()


def norm_rows(mine_ref, x_ref, n_ref, xq_ref, turn_ref, arrived):
    count = x_ref.shape[1]
    to = lax.broadcasted_iota(jnp.int32, turn_ref.shape, 0)
    source = lax.broadcasted_iota(jnp.int32, turn_ref.shape, 1)
    turn_ref[...] = jnp.where((to & 15) * count + (to >> 4) == source, 1.0, 0.0).astype(BF)
    for b in range(8):
        if 16 * b in arrived:
            arrived[16 * b].wait()
        rows = normed(x_ref[16 * b : 16 * b + 16].astype(F32).reshape(16 * count, D))
        rows = dot(turn_ref[...], rows).astype(BF)
        for u in range(count):
            n_ref[u, 16 * b : 16 * b + 16, :] = rows[16 * u : 16 * u + 16]
    xq_ref[...] = x_ref[pl.ds(mine_ref[0] * 32, 32)]


def prepare_early(mine_ref, frames_ref, n_ref, xq_ref, late_ref, x_ref, turn_ref, sems):
    arrived = {}
    for k, (at, to) in enumerate(((0, 16), (16, 48), (48, 128))):
        part = pl.ds(at, to - at)
        arrived[at] = pltpu.make_async_copy(frames_ref.at[part], x_ref.at[part], sems.at[k])
        arrived[at].start()
    length = K - HALF
    late = pltpu.make_async_copy(
        frames_ref.at[pl.ds(HALF, length)], late_ref.at[pl.ds(0, length)], sems.at[3]
    )
    late.start()
    norm_rows(mine_ref, x_ref, n_ref, xq_ref, turn_ref, arrived)
    late.wait()
    late_ref[length:128] = late_ref[length - (128 - length) : length]


def prepare_late(mine_ref, x_ref, n_ref, xq_ref, turn_ref):
    norm_rows(mine_ref, x_ref, n_ref, xq_ref, turn_ref, {})


def intra_attention(mine_ref, early_ref, late_ref, w0, w1, w2, w3, o_ref, weights_ref):
    @pl.when(pl.program_id(0) == 0)
    def _():
        put_attention_weights((w0, w1, w2, w3), weights_ref)

    own = pl.multiple_of(mine_ref[0] * 32, 32)
    count = early_ref.shape[0]
    row = lax.broadcasted_iota(jnp.int32, (256, 256), 0)
    lane = lax.broadcasted_iota(jnp.int32, (256, 256), 1)
    same = (row & 127) >> 5 == lane >> 6
    valid = jnp.concatenate([row[0:8] < 5] * 2, axis=1)
    rows, few = [], []
    for u in range(count):
        rows += [early_ref[u], late_ref[u]]
        few += [early_ref[u, pl.ds(own, 32), :], late_ref[u, pl.ds(own, 32), :]] * 4
    rows = jnp.concatenate(rows, axis=0)
    keys = dot(rows, weights_ref[1], 1, 1).astype(BF)
    query = dot(weights_ref[0], jnp.concatenate(few, axis=0), 1, 1) * Q_SCALE
    values = dot(weights_ref[2], rows, 1, 1).astype(BF)
    ones = jnp.ones((16, 256), BF)

    def scores(u):
        at = slice(256 * u, 256 * u + 256)
        own_query = query[:, at]
        low = jnp.where(same & (row < 128), own_query, 0.0)
        high = jnp.where(same & (row >= 128), own_query, 0.0)
        score = dot(keys[at], jnp.concatenate([low, high], axis=1).astype(BF))
        pieces = []
        for at in (0, 128):
            pieces += [score[at : at + 120], jnp.where(valid, score[at + 120 : at + 128], LOW)]
        return jnp.concatenate(pieces, axis=0)

    following = scores(0)
    found = []
    for u in range(count):
        current = following
        if u + 1 < count:
            following = scores(u + 1)
        top = jnp.max(current, axis=0, keepdims=True)
        weights = jnp.exp2(current - top).astype(BF)
        for g in range(2):
            value = values[128 * g : 128 * g + 128, 256 * u : 256 * u + 256]
            mixed = dot(
                jnp.concatenate([value, ones], axis=0), weights[:, 256 * g : 256 * g + 256]
            )
            mixed = jnp.where(same[0:128], mixed[0:128] * (1.0 / mixed[128:129]), 0.0)
            mixed = (mixed[:, 0:128] + mixed[:, 128:256]).T
            found.append((mixed[0:64] + mixed[64:128]).astype(BF))
    for u in range(count):
        o_ref[u] = jnp.concatenate(found[2 * u : 2 * u + 2], axis=1)


def add_hidden(rows, total, up, down):
    hidden = jnp.maximum(dot(rows, up[0]), 0.0).astype(BF)
    for k in range(len(up)):
        ready = hidden
        if k + 1 < len(up):
            hidden = jnp.maximum(dot(rows, up[k + 1]), 0.0).astype(BF)
        total = total + dot(ready, down[k])
    return total


def feed_forward(middles, up, down):
    done = []
    following = normed(middles[0].astype(F32))
    for at, middle in enumerate(middles):
        rows = following
        if at + 1 < len(middles):
            following = normed(middles[at + 1].astype(F32))
        done.append((rows, add_hidden(rows, middle.astype(F32), up, down)))
    return done


def intra_feed_forward(a_ref, xq0_ref, xq1_ref, f0, f1, f2, f3, w0, rows_ref, total_ref):
    shards = (w0,)
    count = xq0_ref.shape[1]
    out = jnp.concatenate([w[192:256, :] for w in (f0, f1, f2, f3)], axis=0)
    up = [w[768:1024, :] for w in shards]
    down = [w[1024:1280, :] for w in shards]
    turn = swapped(count, 3)
    middles = []
    for half in range(2):
        for pair in range(2):
            rows = []
            for at in (32 * half + 16 * pair, 32 * half + 16 * pair + 8):
                taken = [a_ref[u, at : at + 8, :].astype(F32) for u in range(count)]
                rows.append(dot(turn, jnp.concatenate(taken, axis=0).astype(BF)).astype(BF))
            x = (xq0_ref, xq1_ref)[half][16 * pair : 16 * pair + 16].astype(F32).reshape(16 * count, D)
            middles.append((x + dot(jnp.concatenate(rows, axis=0), out)).astype(BF))
    size = 16 * count
    for at, (rows, total) in enumerate(feed_forward(middles, up, down)):
        rows_ref[size * at : size * at + size, :] = rows
        total_ref[size * at : size * at + size, :] = total


def intra_more_hidden(rows_ref, total_ref, w1, w2, o_ref):
    size = rows_ref.shape[0] // 4
    up = [w[768:1024, :] for w in (w1, w2)]
    down = [w[1024:1280, :] for w in (w1, w2)]
    for at in (slice(size * k, size * k + size) for k in range(4)):
        o_ref[at] = add_hidden(rows_ref[at], total_ref[at], up, down)


def intra_last_hidden(rows_ref, total_ref, w_ref, o_ref):
    count = o_ref.shape[2]
    size = 16 * count
    for half in range(2):
        for pair in range(2):
            at = slice(size * (2 * half + pair), size * (2 * half + pair + 1))
            total = add_hidden(
                rows_ref[at], total_ref[at], [w_ref[768:1024, :]], [w_ref[1024:1280, :]]
            )
            total = total.astype(BF).astype(F32).reshape(16, count, D)
            o_ref[16 * pair : 16 * pair + 16, half] = total.astype(BF)


def inter_layer(x_ref, w0, w1, w2, w3, o_ref, weights_ref, query_ref, key_ref, value_ref, attended_ref, later_ref):
    shards = (w0, w1, w2, w3)
    put_attention_weights(shards, weights_ref)
    for half in (1, 0):
        x = x_ref[:, half].astype(F32).reshape(later_ref.shape)
        project(normed(x), weights_ref, query_ref, key_ref, value_ref)
        attend(query_ref, key_ref, value_ref, attended_ref)
        attended = attended_ref[...].T.astype(BF)
        middle = (x + dot(attended, weights_ref[3])).astype(BF)
        done = feed_forward(
            [middle[at : at + 256] for at in range(0, x.shape[0], 256)],
            [w[256:512, :] for w in shards],
            [w[512:768, :] for w in shards],
        )
        done = jnp.concatenate([total.astype(BF) for _, total in done], axis=0)
        if half == 1:
            first = lax.broadcasted_iota(jnp.int32, done.shape, 0) == 0
            later_ref[...] = jnp.where(first, 0.0, pltpu.roll(done.astype(F32), 1, 0))
        else:
            summed = (done.astype(F32) + later_ref[...]).reshape(x_ref.shape[0], *x_ref.shape[2:])
            for copy in range(2):
                o_ref[:, copy] = summed.astype(BF)


def assemble(mine_ref, p0, p1, o_ref, rows_ref, done_ref, sems):
    turn = swapped(32, 3)
    for piece, core, z in ((p, core, z) for core, p in enumerate((p0, p1)) for z in range(2)):
        at = pl.multiple_of((2 * z + ((mine_ref[0] & 1) ^ core)) * 32, 32)
        for part in range(3):
            taken = [piece[2 * s + z, 8 * part : 8 * part + 8, :].astype(F32) for s in range(32)]
            rows = dot(turn, jnp.concatenate(taken, axis=0).astype(BF)).astype(BF)
            for u in range(8):
                rows_ref[8 * part + u, pl.ds(at, 32), :] = rows[32 * u : 32 * u + 32]
    to = lax.broadcasted_iota(jnp.int32, (128, 256), 0)
    source = lax.broadcasted_iota(jnp.int32, (128, 256), 1)
    copies = []
    for b in range(24):
        place = to + 3 * b
        place = jnp.where(place < HALF, place, place + 3)
        pick = jnp.where(place == source, 1.0, 0.0).astype(BF)
        rows = jnp.concatenate([rows_ref[b], rows_ref[min(b + 1, 23)]], axis=0)
        size = min(128, 3000 - 128 * b)
        done_ref[128 * b : 128 * b + size, :] = dot(pick, rows)[0:size].astype(BF)
        if b % 4 == 3:
            part = pl.ds(128 * (b - 3), 384 + size)
            copies.append(
                pltpu.make_async_copy(done_ref.at[part], o_ref.at[part], sems.at[b // 4])
            )
            copies[-1].start()
    for copy in copies:
        copy.wait()


def whole(shape):
    return pl.BlockSpec(shape, lambda i, *_: (0,) * len(shape))


def attention_scratch(length):
    return [
        pltpu.VMEM((4, D, D), BF),
        pltpu.VMEM((D, length), BF),
        pltpu.VMEM((HEADS, length, 128), BF),
        pltpu.VMEM((HEADS, 48, length), BF),
        pltpu.VMEM((D, length), F32),
    ]


def by(shard, k):
    return lax.ppermute(shard, "mp", [(i, i ^ k) for i in range(MP)])


def on_device(
    frames, intra_qkv, intra_out, intra_up, intra_down, inter_qkv, inter_out, inter_up, inter_down
):
    seq_count = lax.axis_size("seq")
    mine = lax.axis_index("mp").reshape(1)
    count = frames.shape[0]
    total = count * seq_count

    weights = (
        jnp.transpose(intra_qkv, (1, 2, 0)).reshape(-1, D),
        intra_out,
        jnp.transpose(inter_qkv, (1, 2, 0)).reshape(-1, D),
        inter_out,
        inter_up,
        inter_down,
        intra_up,
        intra_down,
    )
    first, rest = pl.pallas_call(
        functools.partial(pack, 2),
        out_shape=(jax.ShapeDtypeStruct((256, D), BF), jax.ShapeDtypeStruct((1280, D), BF)),
        in_specs=[IN_HBM] * len(weights),
        out_specs=[IN_VMEM] * 2,
        scratch_shapes=[pltpu.SemaphoreType.DMA((len(weights),))],
        compiler_params=params(4),
        name="pack",
    )(*[pltpu.with_memory_space_constraint(a, pltpu.HBM) for a in weights])
    across = by(first, 2)
    first = [first, by(first, 1), across, by(across, 1)]

    halves = (
        jax.ShapeDtypeStruct((count, 128, D), BF),
        jax.ShapeDtypeStruct((32, count, D), BF),
        jax.ShapeDtypeStruct((128, count, D), BF),
    )
    turn = pltpu.VMEM((16 * count, 16 * count), BF)
    early, early_frames, late_stored = pl.pallas_call(
        prepare_early,
        out_shape=halves,
        grid_spec=pltpu.PrefetchScalarGridSpec(
            num_scalar_prefetch=1,
            in_specs=[IN_HBM],
            out_specs=[IN_VMEM] * 3,
            scratch_shapes=[
                pltpu.VMEM((128, count, D), BF),
                turn,
                pltpu.SemaphoreType.DMA((4,)),
            ],
        ),
        compiler_params=params(16),
        cost_estimate=pl.CostEstimate(flops=10**9, bytes_accessed=4 * 10**6, transcendentals=10**4),
        name="prepare_early",
    )(mine, pltpu.with_memory_space_constraint(jnp.transpose(frames, (1, 0, 2)), pltpu.HBM))
    rest, first[2], early = lax.optimization_barrier((rest, across, early))
    rest = [rest, None, by(rest, 2)]
    late, late_frames = pl.pallas_call(
        prepare_late,
        out_shape=halves[:2],
        grid_spec=pltpu.PrefetchScalarGridSpec(
            num_scalar_prefetch=1,
            in_specs=[IN_VMEM],
            out_specs=[IN_VMEM] * 2,
            scratch_shapes=[turn],
        ),
        compiler_params=params(16),
        cost_estimate=pl.CostEstimate(flops=10**8, bytes_accessed=10**5, transcendentals=10**4),
        name="prepare_late",
    )(mine, late_stored)
    rows, own_frames = (early, late), (early_frames, late_frames)

    group = 12
    attended = pl.pallas_call(
        intra_attention,
        out_shape=jax.ShapeDtypeStruct((count, 64, D), BF),
        grid_spec=pltpu.PrefetchScalarGridSpec(
            num_scalar_prefetch=1,
            grid=(count // group,),
            in_specs=[pl.BlockSpec((group, 128, D), lambda i, *_: (i, 0, 0))] * 2
            + [whole((192, D))] * 4,
            out_specs=pl.BlockSpec((group, 64, D), lambda i, *_: (i, 0, 0)),
            scratch_shapes=[pltpu.VMEM((3, D, D), BF)],
        ),
        compiler_params=params(20),
        cost_estimate=pl.CostEstimate(flops=10**9, bytes_accessed=10**6, transcendentals=10**6),
        name="intra_attention",
    )(mine, *rows, *first)

    beside, attended = lax.optimization_barrier((rest[0], attended))
    rest[1] = by(beside, 1)

    normed_rows, partial_sums = pl.pallas_call(
        intra_feed_forward,
        out_shape=(
            jax.ShapeDtypeStruct((64 * count, D), BF),
            jax.ShapeDtypeStruct((64 * count, D), F32),
        ),
        in_specs=[IN_VMEM] * 8,
        out_specs=[IN_VMEM] * 2,
        compiler_params=params(24),
        cost_estimate=pl.CostEstimate(flops=10**8, bytes_accessed=10**5, transcendentals=0),
        name="intra_feed_forward",
    )(attended, *own_frames, *first, rest[0])
    rest[2], partial_sums = lax.optimization_barrier((rest[2], partial_sums))
    rest.append(by(rest[2], 1))
    partial_sums = pl.pallas_call(
        intra_more_hidden,
        out_shape=jax.ShapeDtypeStruct((64 * count, D), F32),
        in_specs=[IN_VMEM] * 4,
        out_specs=IN_VMEM,
        input_output_aliases={1: 0},
        compiler_params=params(16),
        cost_estimate=pl.CostEstimate(flops=10**9, bytes_accessed=3 * 10**6, transcendentals=0),
        name="intra_more_hidden",
    )(normed_rows, partial_sums, *rest[1:3])
    sent = pl.pallas_call(
        intra_last_hidden,
        out_shape=jax.ShapeDtypeStruct((seq_count, 2, count, D), BF),
        in_specs=[IN_VMEM] * 3,
        out_specs=IN_VMEM,
        compiler_params=params(16),
        cost_estimate=pl.CostEstimate(flops=10**9, bytes_accessed=3 * 10**6, transcendentals=0),
        name="intra_last_hidden",
    )(normed_rows, partial_sums, rest[3])
    sent = sent.reshape(seq_count, 2 * count, D)
    got = lax.all_to_all(sent, "seq", split_axis=0, concat_axis=0, tiled=True)
    summed = pl.pallas_call(
        inter_layer,
        out_shape=jax.ShapeDtypeStruct((seq_count, 2, count, D), BF),
        in_specs=[IN_VMEM] * 5,
        out_specs=IN_VMEM,
        scratch_shapes=attention_scratch(total) + [pltpu.VMEM((total, D), F32)],
        compiler_params=params(32),
        cost_estimate=pl.CostEstimate(flops=3 * 10**10, bytes_accessed=4 * 10**6, transcendentals=10**7),
        name="inter_layer",
    )(got.reshape(seq_count, 2, count, D), *rest)

    back = summed.reshape(2 * seq_count, count, D)
    chips = [(s, z) for s in range(seq_count) for z in range(2)]
    groups = [[MP * s + 2 * z + core for s, z in chips] for core in range(2)]
    back = lax.all_to_all(
        back, ("seq", "mp"), split_axis=0, concat_axis=0, tiled=True, axis_index_groups=groups
    )
    pieces = [back, by(back, 1)]
    return pl.pallas_call(
        assemble,
        out_shape=jax.ShapeDtypeStruct((HALF * count, D), BF),
        grid_spec=pltpu.PrefetchScalarGridSpec(
            num_scalar_prefetch=1,
            in_specs=[IN_VMEM] * 2,
            out_specs=IN_HBM,
            scratch_shapes=[
                pltpu.VMEM((count, 128, D), BF),
                pltpu.VMEM((HALF * count, D), BF),
                pltpu.SemaphoreType.DMA((6,)),
            ],
        ),
        compiler_params=params(12),
        cost_estimate=pl.CostEstimate(flops=10**9, bytes_accessed=4 * 10**6, transcendentals=0),
        name="assemble",
    )(mine, *pieces)


def solution(mesh):
    return jax.shard_map(
        on_device,
        mesh=mesh,
        in_specs=(
            P("seq", None, None),
            P(None, None, "mp"),
            P("mp", None),
            P(None, "mp"),
            P("mp", None),
            P(None, None, "mp"),
            P("mp", None),
            P(None, "mp"),
            P("mp", None),
        ),
        out_specs=P("seq", None),
        check_vma=False,
    )
```

```python
import functools

import jax
import jax.numpy as jnp
from jax import lax
from jax.experimental import pallas as pl
from jax.experimental.pallas import tpu as pltpu
from jax.sharding import PartitionSpec as P

HEADS = 8
HD = 32
K = 250
HALF = K // 2
D = 256
MP = 4
BF = jnp.bfloat16
F32 = jnp.float32
Q_SCALE = 1.4426950408889634 * HD ** (-0.5)
LOW = -1e30
IN_HBM = pl.BlockSpec(memory_space=pltpu.HBM)
IN_VMEM = pl.BlockSpec(memory_space=pltpu.VMEM)


def params(mebibytes):
    return pltpu.CompilerParams(vmem_limit_bytes=mebibytes * 1024 * 1024)


def dot(left, right, left_dim=1, right_dim=0):
    return lax.dot_general(
        left, right, (((left_dim,), (right_dim,)), ((), ())), preferred_element_type=F32
    )


def normed(values):
    centre = values - jnp.mean(values, axis=-1, keepdims=True)
    spread = jnp.mean(centre * centre, axis=-1, keepdims=True)
    return (centre * lax.rsqrt(spread + 1e-05)).astype(BF)


def put_attention_weights(shards, weights_ref):
    for k in range(MP):
        for t in range(weights_ref.shape[0]):
            weights_ref[t, 64 * k : 64 * k + 64, :] = shards[k][64 * t : 64 * t + 64, :]


def project(rows, weights_ref, query_ref, key_ref, value_ref):
    query_ref[...] = (dot(weights_ref[0], rows, 1, 1) * Q_SCALE).astype(BF)
    keys = dot(rows, weights_ref[1], 1, 1).astype(BF)
    lane = lax.broadcasted_iota(jnp.int32, (rows.shape[0], 128), 1) // HD
    for h in range(HEADS):
        part = keys[:, 128 * (h // 4) : 128 * (h // 4) + 128]
        key_ref[h] = jnp.where(lane == h % 4, part, jnp.zeros_like(part))
    values = dot(weights_ref[2], rows, 1, 1).astype(BF)
    for h in range(HEADS):
        value_ref[h, 0:HD, :] = values[HD * h : HD * h + HD, :]
        value_ref[h, HD:40, :] = jnp.ones((40 - HD, rows.shape[0]), BF)


def attend(query_ref, key_ref, value_ref, attended_ref):
    def scores(h):
        half = 128 * (h // 4)
        return dot(key_ref[h], query_ref[half : half + 128, :])

    following = scores(0)
    for h in range(HEADS):
        current = following
        if h + 1 < HEADS:
            following = scores(h + 1)
        top = jnp.max(current, axis=0, keepdims=True)
        weights = jnp.exp2(current - top).astype(BF)
        mixed = dot(value_ref[h], weights)
        attended_ref[HD * h : HD * h + HD, :] = mixed[0:HD] * (1.0 / mixed[HD : HD + 1])


def swapped(outer, bits):
    inner = 1 << bits
    size = outer * inner
    to = lax.broadcasted_iota(jnp.int32, (size, size), 0)
    source = lax.broadcasted_iota(jnp.int32, (size, size), 1)
    return jnp.where((source & (inner - 1)) * outer + (source >> bits) == to, 1.0, 0.0).astype(BF)


def pack(early, *refs):
    sources, (first_ref, rest_ref, sems) = refs[:-3], refs[-3:]
    copies = []
    for some, into in ((range(early), first_ref), (range(early, len(sources)), rest_ref)):
        at = 0
        for k in some:
            size = sources[k].shape[0]
            copies.append(pltpu.make_async_copy(sources[k], into.at[pl.ds(at, size)], sems.at[k]))
            copies[-1].start()
            at += size
    for copy in copies:
        copy.wait()


def norm_rows(mine_ref, x_ref, n_ref, xq_ref, turn_ref, arrived):
    count = x_ref.shape[1]
    to = lax.broadcasted_iota(jnp.int32, turn_ref.shape, 0)
    source = lax.broadcasted_iota(jnp.int32, turn_ref.shape, 1)
    turn_ref[...] = jnp.where((to & 15) * count + (to >> 4) == source, 1.0, 0.0).astype(BF)
    for b in range(8):
        if 16 * b in arrived:
            arrived[16 * b].wait()
        rows = normed(x_ref[16 * b : 16 * b + 16].astype(F32).reshape(16 * count, D))
        rows = dot(turn_ref[...], rows).astype(BF)
        for u in range(count):
            n_ref[u, 16 * b : 16 * b + 16, :] = rows[16 * u : 16 * u + 16]
    xq_ref[...] = x_ref[pl.ds(mine_ref[0] * 32, 32)]


def prepare_early(mine_ref, frames_ref, n_ref, xq_ref, late_ref, x_ref, turn_ref, sems):
    arrived = {}
    for k, (at, to) in enumerate(((0, 16), (16, 48), (48, 128))):
        part = pl.ds(at, to - at)
        arrived[at] = pltpu.make_async_copy(frames_ref.at[part], x_ref.at[part], sems.at[k])
        arrived[at].start()
    length = K - HALF
    late = pltpu.make_async_copy(
        frames_ref.at[pl.ds(HALF, length)], late_ref.at[pl.ds(0, length)], sems.at[3]
    )
    late.start()
    norm_rows(mine_ref, x_ref, n_ref, xq_ref, turn_ref, arrived)
    late.wait()
    late_ref[length:128] = late_ref[length - (128 - length) : length]


def prepare_late(mine_ref, x_ref, n_ref, xq_ref, turn_ref):
    norm_rows(mine_ref, x_ref, n_ref, xq_ref, turn_ref, {})


def intra_attention(mine_ref, early_ref, late_ref, w0, w1, w2, w3, o_ref, weights_ref):
    @pl.when(pl.program_id(0) == 0)
    def _():
        put_attention_weights((w0, w1, w2, w3), weights_ref)

    own = pl.multiple_of(mine_ref[0] * 32, 32)
    count = early_ref.shape[0]
    row = lax.broadcasted_iota(jnp.int32, (256, 256), 0)
    lane = lax.broadcasted_iota(jnp.int32, (256, 256), 1)
    same = (row & 127) >> 5 == lane >> 6
    valid = jnp.concatenate([row[0:8] < 5] * 2, axis=1)
    rows, few = [], []
    for u in range(count):
        rows += [early_ref[u], late_ref[u]]
        few += [early_ref[u, pl.ds(own, 32), :], late_ref[u, pl.ds(own, 32), :]] * 4
    rows = jnp.concatenate(rows, axis=0)
    keys = dot(rows, weights_ref[1], 1, 1).astype(BF)
    query = dot(weights_ref[0], jnp.concatenate(few, axis=0), 1, 1) * Q_SCALE
    values = dot(weights_ref[2], rows, 1, 1).astype(BF)
    ones = jnp.ones((8, 256), BF)

    def scores(u):
        at = slice(256 * u, 256 * u + 256)
        own_query = query[:, at]
        low = jnp.where(same & (row < 128), own_query, 0.0)
        high = jnp.where(same & (row >= 128), own_query, 0.0)
        score = dot(keys[at], jnp.concatenate([low, high], axis=1).astype(BF))
        pieces = []
        for at in (0, 128):
            pieces += [score[at : at + 120], jnp.where(valid, score[at + 120 : at + 128], LOW)]
        return jnp.concatenate(pieces, axis=0)

    following = scores(0)
    found = []
    for u in range(count):
        current = following
        if u + 1 < count:
            following = scores(u + 1)
        top = jnp.max(current, axis=0, keepdims=True)
        weights = jnp.exp2(current - top).astype(BF)
        for g in range(2):
            value = values[128 * g : 128 * g + 128, 256 * u : 256 * u + 256]
            mixed = dot(
                jnp.concatenate([value, ones], axis=0), weights[:, 256 * g : 256 * g + 256]
            )
            mixed = jnp.where(same[0:128], mixed[0:128] * (1.0 / mixed[128:129]), 0.0)
            mixed = (mixed[:, 0:128] + mixed[:, 128:256]).T
            found.append((mixed[0:64] + mixed[64:128]).astype(BF))
    for u in range(count):
        o_ref[u] = jnp.concatenate(found[2 * u : 2 * u + 2], axis=1)


def add_hidden(rows, total, up, down):
    hidden = jnp.maximum(dot(rows, up[0]), 0.0).astype(BF)
    for k in range(len(up)):
        ready = hidden
        if k + 1 < len(up):
            hidden = jnp.maximum(dot(rows, up[k + 1]), 0.0).astype(BF)
        total = total + dot(ready, down[k])
    return total


def feed_forward(middles, up, down):
    done = []
    following = normed(middles[0].astype(F32))
    for at, middle in enumerate(middles):
        rows = following
        if at + 1 < len(middles):
            following = normed(middles[at + 1].astype(F32))
        done.append((rows, add_hidden(rows, middle.astype(F32), up, down)))
    return done


def intra_feed_forward(a_ref, xq0_ref, xq1_ref, f0, f1, f2, f3, w0, rows_ref, total_ref):
    shards = (w0,)
    count = xq0_ref.shape[1]
    out = jnp.concatenate([w[192:256, :] for w in (f0, f1, f2, f3)], axis=0)
    up = [w[768:1024, :] for w in shards]
    down = [w[1024:1280, :] for w in shards]
    turn = swapped(count, 3)
    middles = []
    for half in range(2):
        for pair in range(2):
            rows = []
            for at in (32 * half + 16 * pair, 32 * half + 16 * pair + 8):
                taken = [a_ref[u, at : at + 8, :].astype(F32) for u in range(count)]
                rows.append(dot(turn, jnp.concatenate(taken, axis=0).astype(BF)).astype(BF))
            x = (xq0_ref, xq1_ref)[half][16 * pair : 16 * pair + 16].astype(F32).reshape(16 * count, D)
            middles.append((x + dot(jnp.concatenate(rows, axis=0), out)).astype(BF))
    size = 16 * count
    for at, (rows, total) in enumerate(feed_forward(middles, up, down)):
        rows_ref[size * at : size * at + size, :] = rows
        total_ref[size * at : size * at + size, :] = total


def intra_more_hidden(rows_ref, total_ref, w1, w2, o_ref):
    size = rows_ref.shape[0] // 4
    up = [w[768:1024, :] for w in (w1, w2)]
    down = [w[1024:1280, :] for w in (w1, w2)]
    for at in (slice(size * k, size * k + size) for k in range(4)):
        o_ref[at] = add_hidden(rows_ref[at], total_ref[at], up, down)


def intra_last_hidden(rows_ref, total_ref, w_ref, o_ref):
    count = o_ref.shape[2]
    size = 16 * count
    for half in range(2):
        for pair in range(2):
            at = slice(size * (2 * half + pair), size * (2 * half + pair + 1))
            total = add_hidden(
                rows_ref[at], total_ref[at], [w_ref[768:1024, :]], [w_ref[1024:1280, :]]
            )
            total = total.astype(BF).astype(F32).reshape(16, count, D)
            o_ref[16 * pair : 16 * pair + 16, half] = total.astype(BF)


def inter_layer(x_ref, w0, w1, w2, w3, o_ref, weights_ref, query_ref, key_ref, value_ref, attended_ref, later_ref):
    shards = (w0, w1, w2, w3)
    put_attention_weights(shards, weights_ref)
    for half in (1, 0):
        x = x_ref[:, half].astype(F32).reshape(later_ref.shape)
        project(normed(x), weights_ref, query_ref, key_ref, value_ref)
        attend(query_ref, key_ref, value_ref, attended_ref)
        attended = attended_ref[...].T.astype(BF)
        middle = (x + dot(attended, weights_ref[3])).astype(BF)
        done = feed_forward(
            [middle[at : at + 256] for at in range(0, x.shape[0], 256)],
            [w[256:512, :] for w in shards],
            [w[512:768, :] for w in shards],
        )
        done = jnp.concatenate([total.astype(BF) for _, total in done], axis=0)
        if half == 1:
            first = lax.broadcasted_iota(jnp.int32, done.shape, 0) == 0
            later_ref[...] = jnp.where(first, 0.0, pltpu.roll(done.astype(F32), 1, 0))
        else:
            summed = (done.astype(F32) + later_ref[...]).reshape(x_ref.shape[0], *x_ref.shape[2:])
            for copy in range(2):
                o_ref[:, copy] = summed.astype(BF)


def turn_pieces(piece_ref, o_ref):
    turn = swapped(32, 3)
    for z in range(2):
        for part in range(3):
            taken = [piece_ref[2 * s + z, 8 * part : 8 * part + 8, :].astype(F32) for s in range(32)]
            rows = dot(turn, jnp.concatenate(taken, axis=0).astype(BF)).astype(BF)
            for u in range(8):
                o_ref[z, 8 * part + u] = rows[32 * u : 32 * u + 32]


def assemble(mine_ref, own_ref, p1, o_ref, rows_ref, done_ref, turned_ref, sems):
    turn_pieces(p1, turned_ref)
    for core, source in enumerate((own_ref, turned_ref)):
        for z in range(2):
            at = pl.multiple_of((2 * z + ((mine_ref[0] & 1) ^ core)) * 32, 32)
            for u in range(rows_ref.shape[0]):
                rows_ref[u, pl.ds(at, 32), :] = source[z, u]
    to = lax.broadcasted_iota(jnp.int32, (128, 256), 0)
    source = lax.broadcasted_iota(jnp.int32, (128, 256), 1)
    copies = []
    for b in range(24):
        place = to + 3 * b
        place = jnp.where(place < HALF, place, place + 3)
        pick = jnp.where(place == source, 1.0, 0.0).astype(BF)
        rows = jnp.concatenate([rows_ref[b], rows_ref[min(b + 1, 23)]], axis=0)
        size = min(128, 3000 - 128 * b)
        done_ref[128 * b : 128 * b + size, :] = dot(pick, rows)[0:size].astype(BF)
        if b % 4 == 3:
            part = pl.ds(128 * (b - 3), 384 + size)
            copies.append(
                pltpu.make_async_copy(done_ref.at[part], o_ref.at[part], sems.at[b // 4])
            )
            copies[-1].start()
    for copy in copies:
        copy.wait()


def whole(shape):
    return pl.BlockSpec(shape, lambda i, *_: (0,) * len(shape))


def attention_scratch(length):
    return [
        pltpu.VMEM((4, D, D), BF),
        pltpu.VMEM((D, length), BF),
        pltpu.VMEM((HEADS, length, 128), BF),
        pltpu.VMEM((HEADS, 40, length), BF),
        pltpu.VMEM((D, length), F32),
    ]


def by(shard, k):
    return lax.ppermute(shard, "mp", [(i, i ^ k) for i in range(MP)])


def on_device(
    frames, intra_qkv, intra_out, intra_up, intra_down, inter_qkv, inter_out, inter_up, inter_down
):
    seq_count = lax.axis_size("seq")
    mine = lax.axis_index("mp").reshape(1)
    count = frames.shape[0]
    total = count * seq_count

    weights = (
        jnp.transpose(intra_qkv, (1, 2, 0)).reshape(-1, D),
        intra_out,
        jnp.transpose(inter_qkv, (1, 2, 0)).reshape(-1, D),
        inter_out,
        inter_up,
        inter_down,
        intra_up,
        intra_down,
    )
    first, rest = pl.pallas_call(
        functools.partial(pack, 2),
        out_shape=(jax.ShapeDtypeStruct((256, D), BF), jax.ShapeDtypeStruct((1280, D), BF)),
        in_specs=[IN_HBM] * len(weights),
        out_specs=[IN_VMEM] * 2,
        scratch_shapes=[pltpu.SemaphoreType.DMA((len(weights),))],
        compiler_params=params(4),
        name="pack",
    )(*[pltpu.with_memory_space_constraint(a, pltpu.HBM) for a in weights])
    across = by(first, 2)
    first = [first, by(first, 1), across, by(across, 1)]

    halves = (
        jax.ShapeDtypeStruct((count, 128, D), BF),
        jax.ShapeDtypeStruct((32, count, D), BF),
        jax.ShapeDtypeStruct((128, count, D), BF),
    )
    turn = pltpu.VMEM((16 * count, 16 * count), BF)
    early, early_frames, late_stored = pl.pallas_call(
        prepare_early,
        out_shape=halves,
        grid_spec=pltpu.PrefetchScalarGridSpec(
            num_scalar_prefetch=1,
            in_specs=[IN_HBM],
            out_specs=[IN_VMEM] * 3,
            scratch_shapes=[
                pltpu.VMEM((128, count, D), BF),
                turn,
                pltpu.SemaphoreType.DMA((4,)),
            ],
        ),
        compiler_params=params(16),
        cost_estimate=pl.CostEstimate(flops=10**9, bytes_accessed=4 * 10**6, transcendentals=10**4),
        name="prepare_early",
    )(mine, pltpu.with_memory_space_constraint(jnp.transpose(frames, (1, 0, 2)), pltpu.HBM))
    rest, first[2], early = lax.optimization_barrier((rest, across, early))
    rest = [rest, None, by(rest, 2)]
    late, late_frames = pl.pallas_call(
        prepare_late,
        out_shape=halves[:2],
        grid_spec=pltpu.PrefetchScalarGridSpec(
            num_scalar_prefetch=1,
            in_specs=[IN_VMEM],
            out_specs=[IN_VMEM] * 2,
            scratch_shapes=[turn],
        ),
        compiler_params=params(16),
        cost_estimate=pl.CostEstimate(flops=10**8, bytes_accessed=10**5, transcendentals=10**4),
        name="prepare_late",
    )(mine, late_stored)
    rows, own_frames = (early, late), (early_frames, late_frames)

    group = 12
    attended = pl.pallas_call(
        intra_attention,
        out_shape=jax.ShapeDtypeStruct((count, 64, D), BF),
        grid_spec=pltpu.PrefetchScalarGridSpec(
            num_scalar_prefetch=1,
            grid=(count // group,),
            in_specs=[pl.BlockSpec((group, 128, D), lambda i, *_: (i, 0, 0))] * 2
            + [whole((192, D))] * 4,
            out_specs=pl.BlockSpec((group, 64, D), lambda i, *_: (i, 0, 0)),
            scratch_shapes=[pltpu.VMEM((3, D, D), BF)],
        ),
        compiler_params=params(20),
        cost_estimate=pl.CostEstimate(flops=10**9, bytes_accessed=10**6, transcendentals=10**6),
        name="intra_attention",
    )(mine, *rows, *first)

    beside, attended = lax.optimization_barrier((rest[0], attended))
    rest[1] = by(beside, 1)

    normed_rows, partial_sums = pl.pallas_call(
        intra_feed_forward,
        out_shape=(
            jax.ShapeDtypeStruct((64 * count, D), BF),
            jax.ShapeDtypeStruct((64 * count, D), F32),
        ),
        in_specs=[IN_VMEM] * 8,
        out_specs=[IN_VMEM] * 2,
        compiler_params=params(24),
        cost_estimate=pl.CostEstimate(flops=10**8, bytes_accessed=10**5, transcendentals=0),
        name="intra_feed_forward",
    )(attended, *own_frames, *first, rest[0])
    rest[2], partial_sums = lax.optimization_barrier((rest[2], partial_sums))
    rest.append(by(rest[2], 1))
    partial_sums = pl.pallas_call(
        intra_more_hidden,
        out_shape=jax.ShapeDtypeStruct((64 * count, D), F32),
        in_specs=[IN_VMEM] * 4,
        out_specs=IN_VMEM,
        input_output_aliases={1: 0},
        compiler_params=params(16),
        cost_estimate=pl.CostEstimate(flops=10**9, bytes_accessed=3 * 10**6, transcendentals=0),
        name="intra_more_hidden",
    )(normed_rows, partial_sums, *rest[1:3])
    sent = pl.pallas_call(
        intra_last_hidden,
        out_shape=jax.ShapeDtypeStruct((seq_count, 2, count, D), BF),
        in_specs=[IN_VMEM] * 3,
        out_specs=IN_VMEM,
        compiler_params=params(16),
        cost_estimate=pl.CostEstimate(flops=10**9, bytes_accessed=3 * 10**6, transcendentals=0),
        name="intra_last_hidden",
    )(normed_rows, partial_sums, rest[3])
    sent = sent.reshape(seq_count, 2 * count, D)
    got = lax.all_to_all(sent, "seq", split_axis=0, concat_axis=0, tiled=True)
    summed = pl.pallas_call(
        inter_layer,
        out_shape=jax.ShapeDtypeStruct((seq_count, 2, count, D), BF),
        in_specs=[IN_VMEM] * 5,
        out_specs=IN_VMEM,
        scratch_shapes=attention_scratch(total) + [pltpu.VMEM((total, D), F32)],
        compiler_params=params(32),
        cost_estimate=pl.CostEstimate(flops=3 * 10**10, bytes_accessed=4 * 10**6, transcendentals=10**7),
        name="inter_layer",
    )(got.reshape(seq_count, 2, count, D), *rest)

    back = summed.reshape(2 * seq_count, count, D)
    chips = [(s, z) for s in range(seq_count) for z in range(2)]
    groups = [[MP * s + 2 * z + core for s, z in chips] for core in range(2)]
    back = lax.all_to_all(
        back, ("seq", "mp"), split_axis=0, concat_axis=0, tiled=True, axis_index_groups=groups
    )
    own = pl.pallas_call(
        turn_pieces,
        out_shape=jax.ShapeDtypeStruct((2, count, 32, D), BF),
        in_specs=[IN_VMEM],
        out_specs=IN_VMEM,
        compiler_params=params(8),
        cost_estimate=pl.CostEstimate(flops=10**8, bytes_accessed=10**6, transcendentals=0),
        name="turn_pieces",
    )(back)
    pieces = [own, by(back, 1)]
    return pl.pallas_call(
        assemble,
        out_shape=jax.ShapeDtypeStruct((HALF * count, D), BF),
        grid_spec=pltpu.PrefetchScalarGridSpec(
            num_scalar_prefetch=1,
            in_specs=[IN_VMEM] * 2,
            out_specs=IN_HBM,
            scratch_shapes=[
                pltpu.VMEM((count, 128, D), BF),
                pltpu.VMEM((HALF * count, D), BF),
                pltpu.VMEM((2, count, 32, D), BF),
                pltpu.SemaphoreType.DMA((6,)),
            ],
        ),
        compiler_params=params(12),
        cost_estimate=pl.CostEstimate(flops=10**9, bytes_accessed=4 * 10**6, transcendentals=0),
        name="assemble",
    )(mine, *pieces)


def solution(mesh):
    return jax.shard_map(
        on_device,
        mesh=mesh,
        in_specs=(
            P("seq", None, None),
            P(None, None, "mp"),
            P("mp", None),
            P(None, "mp"),
            P("mp", None),
            P(None, None, "mp"),
            P("mp", None),
            P(None, "mp"),
            P("mp", None),
        ),
        out_specs=P("seq", None),
        check_vma=False,
    )
```
